32 devices in a mesh: section: 2 (over core), ctx: 4 (over z), tp: 4 (over y, x).
Axes of the slice: x: 2, y: 2, z: 4, core: 2. Of those that a mesh axis runs over, the one named last changes fastest.
Arguments:
- q_raw: bfloat16 [2048, 3072], P(('section', 'ctx'), 'tp'), may hold values from -8000 to 8000
- k_raw: bfloat16 [2048, 3072], P(('section', 'ctx'), 'tp'), may hold values from -8000 to 8000
- values: bfloat16 [2048, 3072], P(('section', 'ctx'), 'tp'), may hold values from -6 to 6
- text_k: bfloat16 [512, 3072], P(('section', 'ctx'), 'tp'), may hold values from -8000 to 8000
- text_v: bfloat16 [512, 3072], P(('section', 'ctx'), 'tp'), may hold values from -6 to 6
- q_gain: float32 [3072], P('tp'), may hold values from 0.4 to 1.6
- k_gain: float32 [3072], P('tp'), may hold values from 0.4 to 1.6
- cotangent: bfloat16 [2048, 3072], P(('section', 'ctx'), 'tp'), may hold values from -80 to 80
- vid_len: int32 [1], replicated, may hold values from 1024 to 2048
- txt_len: int32 [1], replicated, may hold values from 384 to 512
Outputs:
- attention_out: bfloat16 [2048, 3072], P(('section', 'ctx'), 'tp')
- d_q_raw: bfloat16 [2048, 3072], P(('section', 'ctx'), 'tp')
- d_k_raw: bfloat16 [2048, 3072], P(('section', 'ctx'), 'tp')
- d_values: bfloat16 [2048, 3072], P(('section', 'ctx'), 'tp')
- d_text_k: bfloat16 [512, 3072], P(('section', 'ctx'), 'tp')
- d_text_v: bfloat16 [512, 3072], P(('section', 'ctx'), 'tp')
- d_q_gain: float32 [3072], P('tp')
- d_k_gain: float32 [3072], P('tp')
The draws below stay inside these ranges and needn't reach their ends.
All inputs are finite; a program needn't handle non-finite values.
Results may differ from the reference program's by a relative error of at most 0.03.
Values may be sent and summed in bfloat16 or wider, within the bound.
No kernel may reach another device: no remote copies, remote signals or barrier semaphores. Data moves between devices by JAX's collectives and lax.ppermute only.
A program may use at most 64 MiB of HBM per device.

```python
import jax
import jax.numpy as jnp
from jax import lax

HD = 128
HEADS = 24
DW = 3072
S_TXT = 512
TOKENS = 2048


def column_scales(key, width):
    jitter = jax.random.uniform(key, (width,), jnp.float32)
    exponent = jitter
    return 10.0 ** exponent


def feature_rows(key, rows):
    base = jnp.clip(jax.random.normal(jax.random.fold_in(key, 1), (rows, DW), jnp.float32), -6.0, 6.0)
    columns = column_scales(jax.random.fold_in(key, 2), DW)
    row_scale = jnp.exp(jax.random.uniform(jax.random.fold_in(key, 3), (rows,), jnp.float32, 0.0, 2.302585))
    return base * columns[None, :] * row_scale[:, None]


def query_key_pair(key):
    queries = feature_rows(jax.random.fold_in(key, 11), TOKENS)
    keys = feature_rows(jax.random.fold_in(key, 12), TOKENS)
    return (queries, keys)


def draw_q_raw(key, part):
    return query_key_pair(key)[0].astype(jnp.bfloat16)


def draw_k_raw(key, part):
    return query_key_pair(key)[1].astype(jnp.bfloat16)


def draw_text_k(key, part):
    return feature_rows(jax.random.fold_in(key, 21), S_TXT).astype(jnp.bfloat16)


def draw_cotangent(key, part):
    position = jnp.arange(TOKENS, dtype=jnp.float32) / TOKENS
    base = jnp.clip(jax.random.normal(jax.random.fold_in(key, 31), (TOKENS, DW), jnp.float32), -6.0, 6.0)
    field = base * (3.0 ** position)[:, None]
    return field.astype(jnp.bfloat16)


def block_levels(rng, extent, split, smallest, high):
    def one(dim, blocks):
        heights = jax.random.uniform(jax.random.fold_in(jax.random.fold_in(rng, 6), dim), (blocks,), jnp.float32, smallest / len(split), high / len(split))
        return jnp.repeat(jnp.exp(heights), extent[dim] // blocks).reshape((-1,) + (1,) * (len(extent) - dim - 1))

    level = one(*split[0])
    for cut in split[1:]:
        level = level * one(*cut)
    return level


def gaussian(own_key, dims, spread, bound, split=(), kind=jnp.bfloat16):
    loudness = block_levels(own_key, dims, split, -0.22, 0.18) if split else 1.0
    drawn = jax.random.normal(own_key, dims, jnp.float32) * spread * loudness
    return jnp.minimum(jnp.maximum(drawn, -bound), bound).astype(kind)


def setup_inputs(seed: int = 0) -> dict:
    arg_keys = jax.random.split(jax.random.key(seed), 11)
    q_raw = draw_q_raw(jax.random.fold_in(arg_keys[10], 71), 0)
    k_raw = draw_k_raw(jax.random.fold_in(arg_keys[10], 71), 0)
    values = gaussian(arg_keys[2], (TOKENS, DW), 1.0, 6.0, ((0, 8), (1, 4)))
    text_k = draw_text_k(jax.random.fold_in(arg_keys[10], 71), 0)
    text_v = gaussian(arg_keys[4], (S_TXT, DW), 1.0, 6.0, ((0, 8), (1, 4)))
    q_gain = jnp.clip(1.0 + 0.12 * jax.random.normal(arg_keys[5], (DW,), jnp.float32), 0.4, 1.6)
    k_gain = jnp.clip(1.0 + 0.12 * jax.random.normal(arg_keys[6], (DW,), jnp.float32), 0.4, 1.6)
    cotangent = draw_cotangent(jax.random.fold_in(arg_keys[10], 71), 0)
    vid_len = jax.random.randint(arg_keys[8], (1,), TOKENS // 2, TOKENS + 1).astype(jnp.int32)
    txt_len = jax.random.randint(arg_keys[9], (1,), 3 * S_TXT // 4, S_TXT + 1).astype(jnp.int32)
    return {"q_raw": q_raw, "k_raw": k_raw, "values": values, "text_k": text_k, "text_v": text_v, "q_gain": q_gain, "k_gain": k_gain, "cotangent": cotangent, "vid_len": vid_len, "txt_len": txt_len}


EPS = 1e-06
NEG = -1e+30

def normed(raw, gain):
    raw_float = raw.astype(jnp.float32)
    factor = lax.rsqrt(lax.optimization_barrier(jnp.sum(raw_float * raw_float, axis=1, keepdims=True)) / DW + EPS)
    return (raw_float, factor, (raw_float * factor * gain).astype(jnp.bfloat16))

def unnormed(raw_float, factor, gain, grad_normed):
    scaled = grad_normed * gain
    total = lax.optimization_barrier(jnp.sum(raw_float * scaled, axis=1, keepdims=True))
    return (factor * scaled - raw_float * factor ** 3 * total / DW).astype(jnp.bfloat16)

def split_heads(matrix):
    return matrix.reshape(matrix.shape[0], HEADS, HD).transpose(1, 0, 2)

def join_heads(stacked):
    return stacked.transpose(1, 0, 2).reshape(stacked.shape[1], DW)

def reference(q_raw, k_raw, values, text_k, text_v, q_gain, k_gain, cotangent, vid_len, txt_len):
    scale = HD ** (-0.5)
    q_float, q_scale, q_normed = normed(q_raw, q_gain)
    k_float, k_scale, k_normed = normed(k_raw, k_gain)
    t_float, t_scale, t_normed = normed(text_k, k_gain)
    keys = jnp.concatenate([k_normed, t_normed], axis=0)
    vals = jnp.concatenate([values, text_v], axis=0)
    live_keys = jnp.concatenate([jnp.arange(TOKENS, dtype=jnp.int32) < vid_len[0], jnp.arange(S_TXT, dtype=jnp.int32) < txt_len[0]])
    live_rows = jnp.arange(TOKENS, dtype=jnp.int32) < vid_len[0]
    grad_out = jnp.where(live_rows[:, None], cotangent, jnp.zeros_like(cotangent))

    def one_head(items):
        query, key, value, grad = items
        scores = jnp.dot(query, key.T, preferred_element_type=jnp.float32) * scale
        scores = jnp.where(live_keys[None, :], scores, NEG)
        row_max = lax.optimization_barrier(jnp.max(scores, axis=1, keepdims=True))
        expos = jnp.where(live_keys[None, :], jnp.exp(scores - row_max), 0.0)
        totals = lax.optimization_barrier(jnp.sum(expos, axis=1, keepdims=True))
        attention = jnp.dot(expos.astype(jnp.bfloat16), value, preferred_element_type=jnp.float32) / totals
        log_total = row_max + jnp.log(totals)
        inner = lax.optimization_barrier(jnp.sum(grad.astype(jnp.float32) * attention, axis=1, keepdims=True))
        probs = jnp.where(live_keys[None, :], jnp.exp(scores - log_total), 0.0)
        value_grad = jnp.dot(probs.astype(jnp.bfloat16).T, grad, preferred_element_type=jnp.float32)
        prob_grad = jnp.dot(grad, value.T, preferred_element_type=jnp.float32)
        score_grad = (probs * (prob_grad - inner) * scale).astype(jnp.bfloat16)
        query_grad = jnp.dot(score_grad, key, preferred_element_type=jnp.float32)
        key_grad = jnp.dot(score_grad.T, query, preferred_element_type=jnp.float32)
        return (attention, query_grad, key_grad, value_grad)
    attention, query_grad, key_grad, value_grad = lax.map(one_head, (split_heads(q_normed), split_heads(keys), split_heads(vals), split_heads(grad_out)))
    attention = join_heads(attention)
    query_grad = join_heads(query_grad)
    key_grad = join_heads(key_grad)
    value_grad = join_heads(value_grad)
    attention_out = jnp.where(live_rows[:, None], attention, 0.0).astype(jnp.bfloat16)
    video_key_grad = key_grad[:TOKENS]
    text_key_grad = key_grad[TOKENS:]
    d_q_raw = unnormed(q_float, q_scale, q_gain, query_grad)
    d_k_raw = unnormed(k_float, k_scale, k_gain, video_key_grad)
    d_text_k = unnormed(t_float, t_scale, k_gain, text_key_grad)
    d_values = value_grad[:TOKENS].astype(jnp.bfloat16)
    d_text_v = value_grad[TOKENS:].astype(jnp.bfloat16)
    d_q_gain = lax.optimization_barrier(jnp.sum(query_grad * q_float * q_scale, axis=0))
    d_k_gain = lax.optimization_barrier(jnp.sum(video_key_grad * k_float * k_scale, axis=0)) + lax.optimization_barrier(jnp.sum(text_key_grad * t_float * t_scale, axis=0))
    return (attention_out, d_q_raw, d_k_raw, d_values, d_text_k, d_text_v, d_q_gain, d_k_gain)
```

```python
import functools

import jax
import jax.numpy as jnp
import numpy as np
from jax import lax
from jax.experimental import pallas as pl
from jax.experimental.pallas import tpu as pltpu
from jax.sharding import PartitionSpec as P

HD = 128
EPS = 1e-06
NEG = -1e30
LOG2E = 1.4426950408889634
GROUP = ("section", "ctx")
BF = jnp.bfloat16
F32 = jnp.float32
GAIN_ROWS = 16


VM = pl.BlockSpec(memory_space=pltpu.VMEM)
SM = pl.BlockSpec(memory_space=pltpu.SMEM)


def head_owners(members, chips, heads):
    order = sorted(range(members), key=lambda d: (abs(2 * (d % chips) - (chips - 1)), d))
    table = np.full((members,), -1, np.int32)
    for head, device in enumerate(order[:heads]):
        table[device] = head
    return table


def columns(head):
    return pl.ds(pl.multiple_of(head * HD, HD), HD)


def tile(i):
    return slice(i * HD, (i + 1) * HD)


def row_to_columns(row):
    return jnp.broadcast_to(row, (HD, row.shape[1])).T


def rows_to_row(block):
    return jnp.sum(block.T, axis=0, keepdims=True)


def nt(a, b):
    return lax.dot_general(a, b, (((1,), (1,)), ((), ())), preferred_element_type=F32)


def nn(a, b):
    return jnp.dot(a, b, preferred_element_type=F32)


def call(kernel, outs, ins, smem=0, scratch=(), flops=0, name=None, aliases=None, vmem=24):
    nbytes = sum(int(np.prod(o.shape)) * o.dtype.itemsize for o in list(outs) + list(ins)[smem:])
    return pl.pallas_call(
        kernel,
        out_shape=tuple(jax.ShapeDtypeStruct(o.shape, o.dtype) for o in outs),
        in_specs=[SM] * smem + [VM] * (len(ins) - smem),
        out_specs=tuple(VM for _ in outs),
        scratch_shapes=list(scratch),
        input_output_aliases=aliases or {},
        compiler_params=pltpu.CompilerParams(vmem_limit_bytes=vmem << 20),
        cost_estimate=pl.CostEstimate(flops=flops, bytes_accessed=nbytes, transcendentals=0),
        name=name,
    )(*ins)


def shaped(shape, dtype):
    return jax.ShapeDtypeStruct(shape, dtype)


def send_v_kernel(me, tab, v, tv, *outs):
    tokens = v.shape[0]
    for r, out in enumerate(outs):
        col = columns(jnp.maximum(tab[me[0] ^ r], 0))
        out[:tokens] = v[:, col]
        out[tokens:] = tv[:, col]


def squares_kernel(q, k, t, out):
    def part(ref):
        total = None
        for i in range(ref.shape[1] // HD):
            x = ref[:, tile(i)].astype(F32)
            total = x * x if total is None else total + x * x
        return total

    parts = [part(q), part(k), part(t)]
    rest = out.shape[1] - sum(p.shape[0] for p in parts)
    if rest:
        parts.append(jnp.zeros((rest, HD), F32))
    out[...] = rows_to_row(jnp.concatenate(parts, axis=0))


def send_k_kernel(width, count, me, tab, *refs):
    sums, (k, tk, gain), outs, scales, normed = (
        refs[:count],
        refs[count : count + 3],
        refs[count + 3 : -2],
        refs[-2],
        refs[-1],
    )
    tokens, texts = k.shape[0], tk.shape[0]
    total = sums[0][...]
    for s in sums[1:]:
        total = total + s[...]
    scale = lax.rsqrt(total * (1.0 / width) + EPS)
    scales[...] = scale
    cols = row_to_columns(scale[:, tokens:])
    for i in range(k.shape[1] // HD):
        g = gain[:, tile(i)]
        normed[:tokens, tile(i)] = (k[:, tile(i)].astype(F32) * cols[:tokens] * g).astype(BF)
        normed[tokens:, tile(i)] = (
            tk[:, tile(i)].astype(F32) * cols[tokens : tokens + texts] * g
        ).astype(BF)
    for r, out in enumerate(outs):
        out[...] = normed[:, columns(jnp.maximum(tab[me[0] ^ r], 0))]


def send_q_kernel(me, tab, vid, scales, q, gain, cot, *refs):
    outs, normed, grad = refs[:-2], refs[-2], refs[-1]
    tokens = q.shape[0]
    cols = row_to_columns(scales[:, :tokens])
    row = me[0] * tokens + lax.broadcasted_iota(jnp.int32, (tokens, HD), 0)
    live = row < vid[0]
    for i in range(q.shape[1] // HD):
        g = gain[:, tile(i)]
        normed[:, tile(i)] = (q[:, tile(i)].astype(F32) * cols * g).astype(BF)
        grad[:, tile(i)] = jnp.where(live, cot[:, tile(i)].astype(F32), 0.0).astype(BF)
    for r, out in enumerate(outs):
        col = columns(jnp.maximum(tab[me[0] ^ r], 0))
        out[:tokens] = normed[:, col]
        out[tokens:] = grad[:, col]


def assemble_kernel(members, texts, me, *refs):
    pieces_v, pieces_k = refs[:members], refs[members : 2 * members]
    k, v, kt, vt = refs[2 * members :]
    tokens = pieces_v[0].shape[0] - texts
    for pieces, whole in ((pieces_k, k), (pieces_v, v)):
        for r in range(members):
            src = me[0] ^ r
            whole[pl.ds(pl.multiple_of(src * texts, texts), texts)] = pieces[r][tokens:]
            start = pl.multiple_of(members * texts + src * tokens, texts)
            whole[pl.ds(start, tokens)] = pieces[r][:tokens]
    for whole, turned in ((k, kt), (v, vt)):
        step = 256
        for start in range(0, whole.shape[0], step):
            turned[:, start : start + step] = whole[start : start + step, :].T


def attention_kernel(spec, me, tab, vid, txt, *refs):
    members, tokens, texts, rounds, first, last, step = spec
    refs = list(refs)
    take = lambda count: [refs.pop(0) for _ in range(count)]
    queries = take(len(rounds))
    k, v, kt, vt = take(4)
    if not first:
        dk_in, dv_in, gain_in = take(3)
    outs = take(len(rounds))
    dk, dv, gains = take(3)
    if last:
        dk_outs, dv_outs = take(members), take(members)
    scores, weights, top, totals, turned_out, turned_dq = take(6)
    scale = HD ** (-0.5)
    span = members * texts
    rows = k.shape[0]

    if first:
        dk[...] = jnp.zeros_like(dk)
        dv[...] = jnp.zeros_like(dv)
        gains[...] = jnp.zeros_like(gains)
    else:
        dk[...] = dk_in[...]
        dv[...] = dv_in[...]
        gains[...] = gain_in[...]

    starts = [(s, True) for s in range(0, span, step)]
    starts += [(s, False) for s in range(span, rows, step)]

    def over_blocks(visit):
        for start, is_text in starts:
            limit = txt[0] - start if is_text else vid[0] - (start - span)

            @pl.when(limit > 0)
            def _():
                visit(slice(start, start + step), limit)

    for query, out, r in zip(queries, outs, rounds, strict=True):
        source = me[0] ^ r
        active = jnp.logical_and(tab[me[0]] >= 0, source * tokens < vid[0])

        @pl.when(jnp.logical_not(active))
        def _():
            out[...] = jnp.zeros_like(out)

        @pl.when(active)
        def _():
            q = query[:tokens]
            grad = query[tokens:]
            top[...] = jnp.full_like(top, NEG)
            totals[...] = jnp.zeros_like(totals)
            turned_out[...] = jnp.zeros_like(turned_out)
            turned_dq[...] = jnp.zeros_like(turned_dq)

            def scan_scores(at, limit):
                s = nt(k[at], q)
                live = lax.broadcasted_iota(jnp.int32, s.shape, 0) < limit
                s = jnp.where(live, s, NEG)
                scores[at] = s
                top[...] = jnp.maximum(
                    top[...], jnp.max(s.reshape(step // 8, 8, tokens), axis=0)
                )

            over_blocks(scan_scores)
            highest = jnp.max(top[...], axis=0, keepdims=True) * (scale * LOG2E)

            def scan_weights(at, limit):
                p = jnp.exp2(scores[at] * (scale * LOG2E) - highest)
                totals[...] += jnp.sum(p.reshape(step // 8, 8, tokens), axis=0)
                low = p.astype(BF)
                weights[at] = low
                turned_out[...] += nn(vt[:, at], low)

            over_blocks(scan_weights)
            inverse = 1.0 / jnp.sum(totals[...], axis=0, keepdims=True)
            attention = turned_out[...] * inverse
            turned_grad = grad.astype(F32).T
            inner = jnp.sum(attention * turned_grad, axis=0, keepdims=True)
            inv_cols = row_to_columns(inverse)
            low_grad = (grad.astype(F32) * inv_cols).astype(BF)
            low_q = (q.astype(F32) * (inv_cols * scale)).astype(BF)
            out[:tokens] = attention.T.astype(BF)

            def scan_grads(at, limit):
                p = weights[at]
                dp = nt(v[at], grad)
                ds = p * (dp - inner).astype(BF)
                dv[at] += nn(p, low_grad)
                dk[at] += nn(ds, low_q)
                turned_dq[...] += nn(kt[:, at], ds)

            over_blocks(scan_grads)
            dq = (turned_dq[...] * (inverse * scale)).T
            out[tokens:] = dq.astype(BF)
            part = dq * q.astype(F32)
            gains[...] += jnp.sum(part.reshape(tokens // 8, 8, HD), axis=0)

    if last:
        gq = jnp.sum(gains[...], axis=0, keepdims=True)
        part = dk[...] * k[...].astype(F32)
        gk = jnp.sum(jnp.sum(part.reshape(rows // 8, 8, HD), axis=0), axis=0, keepdims=True)
        lines = []
        for g in (gq, gk):
            high = g.astype(BF).astype(F32)
            lines += [high, g - high]
        extra = jnp.concatenate(lines + [jnp.zeros((GAIN_ROWS - 4, HD), F32)], axis=0).astype(BF)
        for r in range(members):
            src = me[0] ^ r
            text_at = pl.ds(pl.multiple_of(src * texts, texts), texts)
            video_at = pl.ds(pl.multiple_of(span + src * tokens, texts), tokens)
            for whole, out in ((dk, dk_outs[r]), (dv, dv_outs[r])):
                out[:tokens] = whole[video_at].astype(BF)
                out[tokens : tokens + texts] = whole[text_at].astype(BF)
            dv_outs[r][tokens + texts :] = extra


def gather_q_kernel(members, me, tab, vid, *refs):
    pieces = refs[:members]
    q, gain, out, dq, dots = refs[members:]
    tokens = q.shape[0]
    row = me[0] * tokens + lax.broadcasted_iota(jnp.int32, (tokens, HD), 0)
    live = row < vid[0]
    for r in range(members):
        head = tab[me[0] ^ r]

        @pl.when(head >= 0)
        def _():
            col = columns(jnp.maximum(head, 0))
            out[:, col] = jnp.where(live, pieces[r][:tokens].astype(F32), 0.0).astype(BF)
            dq[:, col] = pieces[r][tokens:]

    total = None
    for i in range(q.shape[1] // HD):
        term = q[:, tile(i)].astype(F32) * (dq[:, tile(i)].astype(F32) * gain[:, tile(i)])
        total = term if total is None else total + term
    dots[...] = rows_to_row(total)


def finish(raw, grads, gain, scale, dots, out, width):
    cols = row_to_columns(scale)
    back = row_to_columns(dots * (scale * scale * scale) * (1.0 / width))
    for i in range(out.shape[1] // HD):
        scaled = grads[:, tile(i)].astype(F32) * gain[:, tile(i)]
        out[:, tile(i)] = (cols * scaled - raw[:, tile(i)].astype(F32) * back).astype(BF)


def total_of(refs):
    total = refs[0][...]
    for ref in refs[1:]:
        total = total + ref[...]
    return total


def finish_q_kernel(width, count, *refs):
    dots = total_of(refs[:count])
    scales, q, dq, gain, out = refs[count:]
    finish(q, dq, gain, scales[:, : q.shape[0]], dots, out, width)


def gather_k_kernel(members, me, tab, *refs):
    pieces = refs[:members]
    k, tk, gain, dk, dots = refs[members:]
    tokens = k.shape[0]
    for r in range(members):
        head = tab[me[0] ^ r]

        @pl.when(head >= 0)
        def _():
            dk[:, columns(jnp.maximum(head, 0))] = pieces[r][...]

    video, text = None, None
    for i in range(k.shape[1] // HD):
        scaled = dk[:, tile(i)].astype(F32) * gain[:, tile(i)]
        a = k[:, tile(i)].astype(F32) * scaled[:tokens]
        b = tk[:, tile(i)].astype(F32) * scaled[tokens:]
        video = a if video is None else video + a
        text = b if text is None else text + b
    parts = [video, text]
    rest = dots.shape[1] - dk.shape[0]
    if rest:
        parts.append(jnp.zeros((rest, HD), F32))
    dots[...] = rows_to_row(jnp.concatenate(parts, axis=0))


def finish_k_kernel(width, count, *refs):
    dots = total_of(refs[:count])
    scales, k, tk, dk, gain, out, text_out = refs[count:]
    tokens = k.shape[0]
    scale = scales[:, tokens:]
    cols = row_to_columns(scale)
    back = row_to_columns(dots * (scale * scale * scale) * (1.0 / width))
    rows = dk.shape[0]
    for i in range(k.shape[1] // HD):
        scaled = dk[:, tile(i)].astype(F32) * gain[:, tile(i)]
        scaled = cols[:rows] * scaled
        out[:, tile(i)] = (
            scaled[:tokens] - k[:, tile(i)].astype(F32) * back[:tokens]
        ).astype(BF)
        text_out[:, tile(i)] = (
            scaled[tokens:] - tk[:, tile(i)].astype(F32) * back[tokens:rows]
        ).astype(BF)


def gather_v_kernel(members, me, tab, *refs):
    pieces = refs[:members]
    q_gain, k_gain, out, text_out, dq_gain, dk_gain = refs[members:]
    tokens, texts = out.shape[0], text_out.shape[0]
    for r in range(members):
        head = tab[me[0] ^ r]

        @pl.when(head >= 0)
        def _():
            col = columns(jnp.maximum(head, 0))
            out[:, col] = pieces[r][:tokens]
            text_out[:, col] = pieces[r][tokens : tokens + texts]
            lines = pieces[r][tokens + texts :].astype(F32)
            dq_gain[:, col] = (lines[0:1] + lines[1:2]) / q_gain[:, col]
            dk_gain[:, col] = (lines[2:3] + lines[3:4]) / k_gain[:, col]


def local(q_raw, k_raw, values, text_k, text_v, q_gain, k_gain, cotangent, vid_len, txt_len):
    tokens, cols = q_raw.shape
    texts = text_k.shape[0]
    heads = cols // HD
    chips = lax.axis_size("ctx")
    members = lax.axis_size(GROUP)
    parts = lax.axis_size("tp")
    width = cols * parts
    table = head_owners(members, chips, heads)
    rounds = range(members)
    keys = members * (tokens + texts)
    pad = -(-(2 * tokens + texts) // HD) * HD

    me = lax.axis_index(GROUP).astype(jnp.int32).reshape(1)
    tab = jnp.asarray(table)
    qg = q_gain.reshape(1, cols)
    kg = k_gain.reshape(1, cols)

    def to_heads(block, r):
        pairs = [(s, s ^ r) for s in range(members) if table[s ^ r] >= 0]
        return block if r == 0 else lax.ppermute(block, GROUP, pairs)

    def to_tokens(block, r):
        pairs = [(s, s ^ r) for s in range(members) if table[s] >= 0]
        return block if r == 0 else lax.ppermute(block, GROUP, pairs)

    def shared(block):
        return [block] + [
            lax.ppermute(block, "tp", [(s, s ^ d) for s in range(parts)]) for d in range(1, parts)
        ]

    bits = lambda c: c.bit_length()
    chip_order = [0] + sorted(range(1, chips), key=lambda c: (-bits(c), c))
    send_order = [c + half * chips for c in chip_order[1:] + [0] for half in (0, 1)]

    vs = call(
        send_v_kernel,
        [shaped((tokens + texts, HD), BF)] * members,
        [me, tab, values, text_v],
        smem=2,
        name="send_v",
    )
    got_v = {r: to_heads(vs[r], r) for r in send_order}

    (sums,) = call(squares_kernel, [shaped((1, pad), F32)], [q_raw, k_raw, text_k], name="squares")
    sums = shared(sums)
    *ks, scales = call(
        functools.partial(send_k_kernel, width, parts),
        [shaped((tokens + texts, HD), BF)] * members + [shaped((1, pad), F32)],
        [me, tab, *sums, k_raw, text_k, kg],
        smem=2,
        scratch=[pltpu.VMEM((tokens + texts, cols), BF)],
        name="send_k",
    )
    got_k = {r: to_heads(ks[r], r) for r in send_order}
    qs = call(
        send_q_kernel,
        [shaped((2 * tokens, HD), BF)] * members,
        [me, tab, vid_len, scales, q_raw, qg, cotangent],
        smem=3,
        scratch=[pltpu.VMEM((tokens, cols), BF)] * 2,
        name="send_q",
    )
    got_q = {r: to_heads(qs[r], r) for r in send_order}

    whole = call(
        functools.partial(assemble_kernel, members, texts),
        [shaped((keys, HD), BF)] * 2 + [shaped((HD, keys), BF)] * 2,
        [me] + [got_v[r] for r in rounds] + [got_k[r] for r in rounds],
        smem=1,
        name="assemble",
    )

    carry = ()
    back_q = {}
    step = 512 if (members * texts) % 512 == 0 else members * texts
    for i, c in enumerate(chip_order):
        mine = (c, c + chips)
        first, last = i == 0, i == chips - 1
        outs = [shaped((2 * tokens, HD), BF)] * 2
        outs += [shaped((keys, HD), F32)] * 2 + [shaped((8, HD), F32)]
        if last:
            outs += [shaped((tokens + texts, HD), BF)] * members
            outs += [shaped((tokens + texts + GAIN_ROWS, HD), BF)] * members
        ins = [me, tab, vid_len, txt_len, *[got_q[r] for r in mine], *whole, *carry]
        result = call(
            functools.partial(
                attention_kernel, (members, tokens, texts, mine, first, last, step)
            ),
            outs,
            ins,
            smem=4,
            scratch=[
                pltpu.VMEM((keys, tokens), F32),
                pltpu.VMEM((keys, tokens), BF),
                pltpu.VMEM((8, tokens), F32),
                pltpu.VMEM((8, tokens), F32),
                pltpu.VMEM((HD, tokens), F32),
                pltpu.VMEM((HD, tokens), F32),
            ],
            flops=6 * 2 * 2 * tokens * keys * HD * 2,
            aliases={} if first else {10: 2, 11: 3, 12: 4},
            name=f"attention_{c}",
        )
        for r, block in zip(mine, result[:2], strict=True):
            back_q[r] = to_tokens(block, r)
        carry = result[2:5]
    dk_parts, dv_parts = result[5 : 5 + members], result[5 + members :]
    back_k = {r: to_tokens(dk_parts[r], r) for r in send_order}
    back_v = {r: to_tokens(dv_parts[r], r) for r in send_order}

    attention_out, dq, dots = call(
        functools.partial(gather_q_kernel, members),
        [shaped((tokens, cols), BF)] * 2 + [shaped((1, tokens), F32)],
        [me, tab, vid_len] + [back_q[r] for r in rounds] + [q_raw, qg],
        smem=3,
        name="gather_q",
    )
    (d_q_raw,) = call(
        functools.partial(finish_q_kernel, width, parts),
        [shaped((tokens, cols), BF)],
        [*shared(dots), scales, q_raw, dq, qg],
        name="finish_q",
    )
    dk, dots = call(
        functools.partial(gather_k_kernel, members),
        [shaped((tokens + texts, cols), BF), shaped((1, pad - tokens), F32)],
        [me, tab] + [back_k[r] for r in rounds] + [k_raw, text_k, kg],
        smem=2,
        name="gather_k",
    )
    d_k_raw, d_text_k = call(
        functools.partial(finish_k_kernel, width, parts),
        [shaped((tokens, cols), BF), shaped((texts, cols), BF)],
        [*shared(dots), scales, k_raw, text_k, dk, kg],
        name="finish_k",
    )
    d_values, d_text_v, d_q_gain, d_k_gain = call(
        functools.partial(gather_v_kernel, members),
        [shaped((tokens, cols), BF), shaped((texts, cols), BF)] + [shaped((1, cols), F32)] * 2,
        [me, tab] + [back_v[r] for r in rounds] + [qg, kg],
        smem=2,
        name="gather_v",
    )
    return (
        attention_out,
        d_q_raw,
        d_k_raw,
        d_values,
        d_text_k,
        d_text_v,
        d_q_gain.reshape(cols),
        d_k_gain.reshape(cols),
    )


def solution(mesh):
    rows = P(GROUP, "tp")
    return jax.shard_map(
        local,
        mesh=mesh,
        in_specs=(rows,) * 5 + (P("tp"), P("tp"), rows, P(), P()),
        out_specs=(rows,) * 6 + (P("tp"), P("tp")),
        check_vma=False,
    )
```

```python
import functools

import jax
import jax.numpy as jnp
import numpy as np
from jax import lax
from jax.experimental import pallas as pl
from jax.experimental.pallas import tpu as pltpu
from jax.sharding import PartitionSpec as P

HD = 128
EPS = 1e-06
NEG = -1e30
LOG2E = 1.4426950408889634
GROUP = ("section", "ctx")
BF = jnp.bfloat16
F32 = jnp.float32


VM = pl.BlockSpec(memory_space=pltpu.VMEM)
SM = pl.BlockSpec(memory_space=pltpu.SMEM)


def head_owners(members, chips, heads):
    order = sorted(range(members), key=lambda d: (abs(2 * (d % chips) - (chips - 1)), d))
    table = np.full((members,), -1, np.int32)
    for head, device in enumerate(order[:heads]):
        table[device] = head
    return table


def columns(head):
    return pl.ds(pl.multiple_of(head * HD, HD), HD)


def tile(i):
    return slice(i * HD, (i + 1) * HD)


def row_to_columns(row):
    return jnp.broadcast_to(row, (HD, row.shape[1])).T


def rows_to_row(block):
    return jnp.sum(block.T, axis=0, keepdims=True)


def nt(a, b):
    return lax.dot_general(a, b, (((1,), (1,)), ((), ())), preferred_element_type=F32)


def nn(a, b):
    return jnp.dot(a, b, preferred_element_type=F32)


def call(kernel, outs, ins, smem=0, scratch=(), flops=0, name=None, aliases=None, vmem=24):
    nbytes = sum(int(np.prod(o.shape)) * o.dtype.itemsize for o in list(outs) + list(ins)[smem:])
    return pl.pallas_call(
        kernel,
        out_shape=tuple(jax.ShapeDtypeStruct(o.shape, o.dtype) for o in outs),
        in_specs=[SM] * smem + [VM] * (len(ins) - smem),
        out_specs=tuple(VM for _ in outs),
        scratch_shapes=list(scratch),
        input_output_aliases=aliases or {},
        compiler_params=pltpu.CompilerParams(vmem_limit_bytes=vmem << 20),
        cost_estimate=pl.CostEstimate(flops=flops, bytes_accessed=nbytes, transcendentals=0),
        name=name,
    )(*ins)


def shaped(shape, dtype):
    return jax.ShapeDtypeStruct(shape, dtype)


def head_at(me, tab, chips, half, c):
    return tab[me[0] ^ (half * chips + c)]


def pack(me, tab, chips, source, mine, other):
    rows = source.shape[0]
    for half, out in ((0, mine), (1, other)):
        for c in range(chips):
            col = columns(jnp.maximum(head_at(me, tab, chips, half, c), 0))
            out[c * rows : (c + 1) * rows] = source[:, col]


def squares(ref):
    total = None
    for i in range(ref.shape[1] // HD):
        x = ref[:, tile(i)].astype(F32)
        total = x * x if total is None else total + x * x
    return total


def first_kernel(chips, me, tab, q_hbm, k_hbm, t_hbm, v_hbm, tv_hbm, mine, other, sums, q, k, t, v, sems):
    tokens = v_hbm.shape[0]
    copies = []
    pairs = [(v_hbm, v.at[:tokens]), (tv_hbm, v.at[tokens:]), (k_hbm, k), (q_hbm, q), (t_hbm, t)]
    for i, (a, b) in enumerate(pairs):
        copies.append(pltpu.make_async_copy(a, b, sems.at[i]))
        copies[-1].start()
    copies[0].wait()
    copies[1].wait()
    pack(me, tab, chips, v, mine, other)
    for copy in copies[2:]:
        copy.wait()
    parts = [squares(q), squares(k), squares(t)]
    rest = sums.shape[1] - sum(p.shape[0] for p in parts)
    if rest:
        parts.append(jnp.zeros((rest, HD), F32))
    sums[...] = rows_to_row(jnp.concatenate(parts, axis=0))


def merge_kernel(chips, mine, other, *outs):
    rows = mine.shape[0] // chips
    for c, out in enumerate(outs):
        out[:rows] = mine[c * rows : (c + 1) * rows]
        out[rows:] = other[c * rows : (c + 1) * rows]


def send_k_kernel(width, count, chips, me, tab, *refs):
    sums, (k, tk, gain, mine, other, scales, normed) = refs[:count], refs[count:]
    tokens, texts = k.shape[0], tk.shape[0]
    scale = lax.rsqrt(total_of(sums) * (1.0 / width) + EPS)
    scales[...] = scale
    cols = row_to_columns(scale[:, tokens:])
    for i in range(k.shape[1] // HD):
        g = gain[:, tile(i)]
        normed[:tokens, tile(i)] = (k[:, tile(i)].astype(F32) * cols[:tokens] * g).astype(BF)
        normed[tokens:, tile(i)] = (
            tk[:, tile(i)].astype(F32) * cols[tokens : tokens + texts] * g
        ).astype(BF)
    pack(me, tab, chips, normed, mine, other)


def send_q_kernel(chips, me, tab, vid, scales, q, gain, cot, mine, other, both):
    tokens = q.shape[0]
    cols = row_to_columns(scales[:, :tokens])
    row = me[0] * tokens + lax.broadcasted_iota(jnp.int32, (tokens, HD), 0)
    live = row < vid[0]
    for i in range(q.shape[1] // HD):
        g = gain[:, tile(i)]
        both[:tokens, tile(i)] = (q[:, tile(i)].astype(F32) * cols * g).astype(BF)
        both[tokens:, tile(i)] = jnp.where(live, cot[:, tile(i)].astype(F32), 0.0).astype(BF)
    pack(me, tab, chips, both, mine, other)


def places(members, tokens, texts, source):
    text_at = pl.ds(pl.multiple_of(source * texts, texts), texts)
    video_at = pl.ds(pl.multiple_of(members * texts + source * tokens, texts), tokens)
    return text_at, video_at


def assemble_kernel(chips, texts, me, *refs):
    pieces_v, pieces_k = refs[:chips], refs[chips : 2 * chips]
    k, v, kt, vt = refs[2 * chips :]
    span = pieces_v[0].shape[0] // 2
    tokens = span - texts
    for pieces, whole in ((pieces_k, k), (pieces_v, v)):
        for c in range(chips):
            for half in (0, 1):
                source = me[0] ^ (half * chips + c)
                text_at, video_at = places(2 * chips, tokens, texts, source)
                whole[text_at] = pieces[c][half * span + tokens : (half + 1) * span]
                whole[video_at] = pieces[c][half * span : half * span + tokens]
    for whole, turned in ((k, kt), (v, vt)):
        step = 256
        for start in range(0, whole.shape[0], step):
            turned[:, start : start + step] = whole[start : start + step, :].T


def attention_kernel(spec, me, tab, vid, txt, *refs):
    chips, tokens, texts, c, first, last, step = spec
    refs = list(refs)
    take = lambda count: [refs.pop(0) for _ in range(count)]
    (query,) = take(1)
    k, v, kt, vt = take(4)
    if not first:
        dk_in, dv_in, gain_in = take(3)
    (out,) = take(1)
    dk, dv, gains = take(3)
    if last:
        (dots,) = take(1)
    scores, weights, top, totals, turned_out, turned_dq = take(6)
    scale = HD ** (-0.5)
    span = 2 * chips * texts
    rows = k.shape[0]

    if first:
        dk[...] = jnp.zeros_like(dk)
        dv[...] = jnp.zeros_like(dv)
        gains[...] = jnp.zeros_like(gains)
    else:
        dk[...] = dk_in[...]
        dv[...] = dv_in[...]
        gains[...] = gain_in[...]

    blocks = span // step + (vid[0] + step - 1) // step

    def over_blocks(visit):
        def body(b, unused):
            start = pl.multiple_of(b * step, step)
            limit = jnp.where(start < span, txt[0] - start, vid[0] - (start - span))
            visit(pl.ds(start, step), limit)
            return unused

        lax.fori_loop(0, blocks, body, 0)

    def piece(half, unused):
        source = me[0] ^ (half * chips + c)
        active = jnp.logical_and(tab[me[0]] >= 0, source * tokens < vid[0])
        q_at = pl.ds(pl.multiple_of(half * 2 * tokens, tokens), tokens)
        grad_at = pl.ds(pl.multiple_of(half * 2 * tokens + tokens, tokens), tokens)

        @pl.when(jnp.logical_not(active))
        def _():
            out[q_at] = jnp.zeros((tokens, HD), BF)
            out[grad_at] = jnp.zeros((tokens, HD), BF)

        @pl.when(active)
        def _():
            q = query[q_at]
            grad = query[grad_at]
            top[...] = jnp.full_like(top, NEG)
            totals[...] = jnp.zeros_like(totals)
            turned_out[...] = jnp.zeros_like(turned_out)
            turned_dq[...] = jnp.zeros_like(turned_dq)

            def scan_scores(at, limit):
                s = nt(k[at], q)
                live = lax.broadcasted_iota(jnp.int32, s.shape, 0) < limit
                s = jnp.where(live, s, NEG)
                scores[at] = s
                top[...] = jnp.maximum(
                    top[...], jnp.max(s.reshape(step // 8, 8, tokens), axis=0)
                )

            over_blocks(scan_scores)
            highest = jnp.max(top[...], axis=0, keepdims=True) * (scale * LOG2E)

            def scan_weights(at, limit):
                p = jnp.exp2(scores[at] * (scale * LOG2E) - highest)
                totals[...] += jnp.sum(p.reshape(step // 8, 8, tokens), axis=0)
                low = p.astype(BF)
                weights[at] = low
                turned_out[...] += nn(vt[:, at], low)

            over_blocks(scan_weights)
            inverse = 1.0 / jnp.sum(totals[...], axis=0, keepdims=True)
            attention = turned_out[...] * inverse
            turned_grad = grad.astype(F32).T
            inner = jnp.sum(attention * turned_grad, axis=0, keepdims=True)
            inv_cols = row_to_columns(inverse)
            low_grad = (grad.astype(F32) * inv_cols).astype(BF)
            low_q = (q.astype(F32) * (inv_cols * scale)).astype(BF)
            out[q_at] = attention.T.astype(BF)

            def scan_grads(at, limit):
                p = weights[at]
                dp = nt(v[at], grad)
                ds = p * (dp - inner).astype(BF)
                dv[at] += nn(p, low_grad)
                dk[at] += nn(ds, low_q)
                turned_dq[...] += nn(kt[:, at], ds)

            over_blocks(scan_grads)
            dq = (turned_dq[...] * (inverse * scale)).T
            out[grad_at] = dq.astype(BF)
            part = dq * q.astype(F32)
            gains[...] += jnp.sum(part.reshape(tokens // 8, 8, HD), axis=0)

        return unused

    lax.fori_loop(0, 2, piece, 0)

    if last:
        for start in range(0, rows, step):
            at = slice(start, start + step)
            part = dk[at] * k[at].astype(F32)
            dots[:, at] = rows_to_row(part)
            gains_k = jnp.sum(part.reshape(step // 8, 8, HD), axis=0)
            if start == 0:
                top[:, :HD] = gains_k
            else:
                top[:, :HD] += gains_k
        gq = jnp.sum(gains[...], axis=0, keepdims=True)
        gk = jnp.sum(top[:, :HD], axis=0, keepdims=True)
        gains[...] = jnp.concatenate([gq, gk, jnp.zeros((6, HD), F32)], axis=0)


def pack_v_kernel(chips, texts, me, dv, *outs):
    span = outs[0].shape[0] // 2
    tokens = span - texts
    for c in range(chips):
        for half in (0, 1):
            source = me[0] ^ (half * chips + c)
            text_at, video_at = places(2 * chips, tokens, texts, source)
            outs[c][half * span : half * span + tokens] = dv[video_at].astype(BF)
            outs[c][half * span + tokens : (half + 1) * span] = dv[text_at].astype(BF)


def pack_k_kernel(chips, texts, count, me, dk, gains, *refs):
    sums, outs, dots = refs[:count], refs[count:-1], refs[-1]
    dots[...] = total_of(sums)
    keys = dk.shape[0]
    text_total = 2 * chips * texts
    tokens = (keys - text_total) // (2 * chips)
    text_lines = [dots[:, tile(i)] for i in range(text_total // HD)]
    gain_lines = [gains[0:1], gains[1:2]]
    for c in range(chips):
        span = outs[c].shape[0] // 2
        for half in (0, 1):
            source = me[0] ^ (half * chips + c)
            text_at, video_at = places(2 * chips, tokens, texts, source)
            base = half * span
            outs[c][base : base + tokens] = dk[video_at].astype(BF)
            outs[c][base + tokens : base + tokens + texts] = dk[text_at].astype(BF)
            lines = list(text_lines) + gain_lines
            for i in range(tokens // HD):
                start = pl.multiple_of(text_total + source * tokens + i * HD, HD)
                lines.append(dots[:, pl.ds(start, HD)])
            block = jnp.concatenate(lines, axis=0)
            high = block.astype(BF).astype(F32)
            both = [high, block - high]
            rest = span - tokens - texts - 2 * block.shape[0]
            if rest:
                both.append(jnp.zeros((rest, HD), F32))
            outs[c][base + tokens + texts : base + span] = jnp.concatenate(both, axis=0).astype(BF)


def split_kernel(chips, *refs):
    out = refs[chips]
    rows = out.shape[0] // chips
    for c in range(chips):
        out[c * rows : (c + 1) * rows] = refs[c][rows:]


def each_head(me, tab, chips, blocks, other, visit):
    rows = other.shape[0] // chips
    for half in (0, 1):
        for c in range(chips):
            head = head_at(me, tab, chips, half, c)

            @pl.when(head >= 0)
            def _():
                col = columns(jnp.maximum(head, 0))
                if half:
                    visit(col, other, c * rows)
                else:
                    visit(col, blocks[c], 0)


def gather_q_kernel(chips, me, tab, vid, *refs):
    blocks, other = refs[:chips], refs[chips]
    q, gain, out, dq, dots = refs[chips + 1 :]
    tokens = q.shape[0]
    row = me[0] * tokens + lax.broadcasted_iota(jnp.int32, (tokens, HD), 0)
    live = row < vid[0]

    def visit(col, ref, at):
        o = ref[at : at + tokens].astype(F32)
        out[:, col] = jnp.where(live, o, 0.0).astype(BF)
        dq[:, col] = ref[at + tokens : at + 2 * tokens]

    each_head(me, tab, chips, blocks, other, visit)
    total = None
    for i in range(q.shape[1] // HD):
        term = q[:, tile(i)].astype(F32) * (dq[:, tile(i)].astype(F32) * gain[:, tile(i)])
        total = term if total is None else total + term
    dots[...] = rows_to_row(total)


def total_of(refs):
    total = refs[0][...]
    for ref in refs[1:]:
        total = total + ref[...]
    return total


def finish_q_kernel(width, count, *refs):
    dots = total_of(refs[:count])
    scales, q, dq, gain, out = refs[count:]
    scale = scales[:, : q.shape[0]]
    cols = row_to_columns(scale)
    back = row_to_columns(dots * (scale * scale * scale) * (1.0 / width))
    for i in range(q.shape[1] // HD):
        scaled = dq[:, tile(i)].astype(F32) * gain[:, tile(i)]
        out[:, tile(i)] = (cols * scaled - q[:, tile(i)].astype(F32) * back).astype(BF)


def gather_v_kernel(chips, me, tab, *refs):
    blocks, other = refs[:chips], refs[chips]
    out, text_out = refs[chips + 1 :]
    tokens, texts = out.shape[0], text_out.shape[0]

    def visit(col, ref, at):
        out[:, col] = ref[at : at + tokens]
        text_out[:, col] = ref[at + tokens : at + tokens + texts]

    each_head(me, tab, chips, blocks, other, visit)


def finish_k_kernel(width, chips, me, tab, *refs):
    blocks, other = refs[:chips], refs[chips]
    scales, k, tk, q_gain, k_gain = refs[chips + 1 : chips + 6]
    out, text_out, dq_gain, dk_gain, dk, sums, text_cols = refs[chips + 6 :]
    tokens, texts = k.shape[0], tk.shape[0]
    text_lines = 2 * chips * texts // HD
    lines = text_lines + 2 + tokens // HD
    sums[...] = jnp.zeros_like(sums)

    def visit(col, ref, at):
        dk[:, col] = ref[at : at + tokens + texts]
        block = ref[at + tokens + texts : at + tokens + texts + 2 * lines].astype(F32)
        block = block[:lines] + block[lines:]
        sums[:lines] += block
        dq_gain[:, col] = block[text_lines : text_lines + 1] / q_gain[:, col]
        dk_gain[:, col] = block[text_lines + 1 : text_lines + 2] / k_gain[:, col]

    each_head(me, tab, chips, blocks, other, visit)
    for i in range(text_lines):
        text_cols[i * HD : (i + 1) * HD] = row_to_columns(sums[i : i + 1])
    scale = scales[:, tokens:]
    cols = row_to_columns(scale)
    text_at = pl.ds(pl.multiple_of(me[0] * texts, texts), texts)
    dots = [row_to_columns(sums[text_lines + 2 + i : text_lines + 3 + i]) for i in range(tokens // HD)]
    dots.append(text_cols[text_at])
    rows = tokens + texts
    back = jnp.concatenate(dots, axis=0) * (cols[:rows] * cols[:rows]) * (1.0 / width)
    for i in range(k.shape[1] // HD):
        scaled = dk[:, tile(i)].astype(F32) * k_gain[:, tile(i)]
        scaled = cols[:rows] * scaled
        out[:, tile(i)] = (scaled[:tokens] - k[:, tile(i)].astype(F32) * back[:tokens]).astype(BF)
        text_out[:, tile(i)] = (
            scaled[tokens:] - tk[:, tile(i)].astype(F32) * back[tokens:]
        ).astype(BF)


def local(q_raw, k_raw, values, text_k, text_v, q_gain, k_gain, cotangent, vid_len, txt_len):
    tokens, cols = q_raw.shape
    texts = text_k.shape[0]
    heads = cols // HD
    chips = lax.axis_size("ctx")
    members = 2 * chips
    parts = lax.axis_size("tp")
    width = cols * parts
    table = head_owners(members, chips, heads)
    span = tokens + texts
    keys = members * span
    text_total = members * texts
    pad = -(-(2 * tokens + texts) // HD) * HD
    extra = -(-2 * (text_total // HD + 2 + tokens // HD) // 16) * 16

    me = lax.axis_index(GROUP).astype(jnp.int32).reshape(1)
    tab = jnp.asarray(table)
    qg = q_gain.reshape(1, cols)
    kg = k_gain.reshape(1, cols)

    def along(block, c, to_owner):
        if c == 0:
            return block
        pairs = [(s, s ^ c) for s in range(members) if table[s ^ c if to_owner else s] >= 0]
        return lax.ppermute(block, GROUP, pairs)

    def sibling(block):
        return lax.ppermute(block, "section", [(0, 1), (1, 0)])

    def shared(block):
        return [block] + [
            lax.ppermute(block, "tp", [(s, s ^ d) for s in range(parts)]) for d in range(1, parts)
        ]

    far_first = sorted(range(1, chips), key=lambda c: (-c.bit_length(), c))
    chip_order = [0] + far_first

    def merged(mine, other, name):
        rows = mine.shape[0] // chips
        messages = call(
            functools.partial(merge_kernel, chips),
            [shaped((2 * rows, HD), BF)] * chips,
            [mine, sibling(other)],
            name=name,
        )
        got = {c: along(messages[c], c, True) for c in far_first}
        got[0] = messages[0]
        return [got[c] for c in range(chips)]

    any_spec = pl.BlockSpec(memory_space=pl.ANY)
    mine_v, other_v, sums = pl.pallas_call(
        functools.partial(first_kernel, chips),
        out_shape=(shaped((chips * span, HD), BF),) * 2 + (shaped((1, pad), F32),),
        in_specs=[SM, SM] + [any_spec] * 5,
        out_specs=(VM,) * 3,
        scratch_shapes=[
            pltpu.VMEM((tokens, cols), BF),
            pltpu.VMEM((tokens, cols), BF),
            pltpu.VMEM((texts, cols), BF),
            pltpu.VMEM((span, cols), BF),
            pltpu.SemaphoreType.DMA((5,)),
        ],
        compiler_params=pltpu.CompilerParams(vmem_limit_bytes=16 << 20),
        name="first",
    )(me, tab, q_raw, k_raw, text_k, values, text_v)
    sums = shared(sums)
    got_v = merged(mine_v, other_v, "merge_v")
    mine_k, other_k, scales = call(
        functools.partial(send_k_kernel, width, parts, chips),
        [shaped((chips * span, HD), BF)] * 2 + [shaped((1, pad), F32)],
        [me, tab, *sums, k_raw, text_k, kg],
        smem=2,
        scratch=[pltpu.VMEM((span, cols), BF)],
        name="send_k",
    )
    got_k = merged(mine_k, other_k, "merge_k")
    mine_q, other_q = call(
        functools.partial(send_q_kernel, chips),
        [shaped((chips * 2 * tokens, HD), BF)] * 2,
        [me, tab, vid_len, scales, q_raw, qg, cotangent],
        smem=3,
        scratch=[pltpu.VMEM((2 * tokens, cols), BF)],
        name="send_q",
    )
    got_q = merged(mine_q, other_q, "merge_q")

    whole = call(
        functools.partial(assemble_kernel, chips, texts),
        [shaped((keys, HD), BF)] * 2 + [shaped((HD, keys), BF)] * 2,
        [me, *got_v, *got_k],
        smem=1,
        name="assemble",
    )

    carry = ()
    back_q = {}
    step = 512
    for i, c in enumerate(chip_order):
        first, last = i == 0, i == chips - 1
        outs = [shaped((4 * tokens, HD), BF)]
        outs += [shaped((keys, HD), F32)] * 2 + [shaped((8, HD), F32)]
        if last:
            outs.append(shaped((1, keys), F32))
        ins = [me, tab, vid_len, txt_len, got_q[c], *whole, *carry]
        result = call(
            functools.partial(attention_kernel, (chips, tokens, texts, c, first, last, step)),
            outs,
            ins,
            smem=4,
            scratch=[
                pltpu.VMEM((keys, tokens), F32),
                pltpu.VMEM((keys, tokens), BF),
                pltpu.VMEM((8, tokens), F32),
                pltpu.VMEM((8, tokens), F32),
                pltpu.VMEM((HD, tokens), F32),
                pltpu.VMEM((HD, tokens), F32),
            ],
            flops=6 * 2 * 2 * tokens * keys * HD * 2,
            aliases={} if first else {9: 1, 10: 2, 11: 3},
            name=f"attention_{c}",
        )
        back_q[c] = along(result[0], c, False)
        carry = result[1:4]
    dk_sum, dv_sum, gains = carry
    dv_parts = call(
        functools.partial(pack_v_kernel, chips, texts),
        [shaped((2 * span, HD), BF)] * chips,
        [me, dv_sum],
        smem=1,
        name="pack_v",
    )
    back_v = {c: along(dv_parts[c], c, False) for c in far_first + [0]}
    dots = shared(result[4])
    dk_parts = call(
        functools.partial(pack_k_kernel, chips, texts, parts),
        [shaped((2 * (span + extra), HD), BF)] * chips,
        [me, dk_sum, gains, *dots],
        smem=1,
        scratch=[pltpu.VMEM((1, keys), F32)],
        name="pack_k",
    )
    back_k = {c: along(dk_parts[c], c, False) for c in far_first + [0]}

    def mine_and_other(back, name):
        blocks = [back[c] for c in range(chips)]
        rows = blocks[0].shape[0] // 2
        (other,) = call(
            functools.partial(split_kernel, chips),
            [shaped((chips * rows, HD), BF)],
            blocks,
            name=name,
        )
        return [*blocks, sibling(other)]

    attention_out, dq, dots_q = call(
        functools.partial(gather_q_kernel, chips),
        [shaped((tokens, cols), BF)] * 2 + [shaped((1, tokens), F32)],
        [me, tab, vid_len, *mine_and_other(back_q, "split_q"), q_raw, qg],
        smem=3,
        name="gather_q",
    )
    (d_q_raw,) = call(
        functools.partial(finish_q_kernel, width, parts),
        [shaped((tokens, cols), BF)],
        [*shared(dots_q), scales, q_raw, dq, qg],
        name="finish_q",
    )
    d_values, d_text_v = call(
        functools.partial(gather_v_kernel, chips),
        [shaped((tokens, cols), BF), shaped((texts, cols), BF)],
        [me, tab, *mine_and_other(back_v, "split_v")],
        smem=2,
        name="gather_v",
    )
    d_k_raw, d_text_k, d_q_gain, d_k_gain = call(
        functools.partial(finish_k_kernel, width, chips),
        [shaped((tokens, cols), BF), shaped((texts, cols), BF)] + [shaped((1, cols), F32)] * 2,
        [me, tab, *mine_and_other(back_k, "split_k"), scales, k_raw, text_k, qg, kg],
        smem=2,
        scratch=[
            pltpu.VMEM((span, cols), BF),
            pltpu.VMEM((extra, HD), F32),
            pltpu.VMEM((text_total, HD), F32),
        ],
        name="finish_k",
    )
    return (
        attention_out,
        d_q_raw,
        d_k_raw,
        d_values,
        d_text_k,
        d_text_v,
        d_q_gain.reshape(cols),
        d_k_gain.reshape(cols),
    )


def solution(mesh):
    rows = P(GROUP, "tp")
    return jax.shard_map(
        local,
        mesh=mesh,
        in_specs=(rows,) * 5 + (P("tp"), P("tp"), rows, P(), P()),
        out_specs=(rows,) * 6 + (P("tp"), P("tp")),
        check_vma=False,
    )
```

```python
import functools

import jax
import jax.numpy as jnp
import numpy as np
from jax import lax
from jax.experimental import pallas as pl
from jax.experimental.pallas import tpu as pltpu
from jax.sharding import PartitionSpec as P


HD = 128
EPS = 1e-06
NEG = -1e30
LOG2E = 1.4426950408889634
GROUP = ("section", "ctx")
BF = jnp.bfloat16
F32 = jnp.float32


VM = pl.BlockSpec(memory_space=pltpu.VMEM)
SM = pl.BlockSpec(memory_space=pltpu.SMEM)


def head_owners(members, chips, heads):
    order = sorted(range(members), key=lambda d: (abs(2 * (d % chips) - (chips - 1)), d))
    table = np.full((members,), -1, np.int32)
    for head, device in enumerate(order[:heads]):
        table[device] = head
    return table


def columns(head):
    return pl.ds(pl.multiple_of(head * HD, HD), HD)


def tile(i):
    return slice(i * HD, (i + 1) * HD)


def row_to_columns(row):
    return jnp.broadcast_to(row, (HD, row.shape[1])).T


def rows_to_row(block):
    return jnp.sum(block.T, axis=0, keepdims=True)


def nt(a, b):
    return lax.dot_general(a, b, (((1,), (1,)), ((), ())), preferred_element_type=F32)


def nn(a, b):
    return jnp.dot(a, b, preferred_element_type=F32)


def call(kernel, outs, ins, smem=0, scratch=(), flops=0, aliases=None, vmem=24, space=None):
    nbytes = sum(int(np.prod(o.shape)) * o.dtype.itemsize for o in list(outs) + list(ins)[smem:])
    big = VM if space is None else space
    return pl.pallas_call(
        kernel,
        out_shape=tuple(jax.ShapeDtypeStruct(o.shape, o.dtype) for o in outs),
        in_specs=[SM] * smem + [big] * (len(ins) - smem),
        out_specs=tuple(VM for _ in outs),
        scratch_shapes=list(scratch),
        input_output_aliases=aliases or {},
        compiler_params=pltpu.CompilerParams(vmem_limit_bytes=vmem << 20),
        cost_estimate=pl.CostEstimate(flops=flops, bytes_accessed=nbytes, transcendentals=0),
    )(*ins)


def shaped(shape, dtype):
    return jax.ShapeDtypeStruct(shape, dtype)


def head_of(tab, device):
    head = jnp.int32(-1)
    for d, h in enumerate(tab):
        if h >= 0:
            head = jnp.where(device == d, jnp.int32(h), head)
    return head


def head_at(me, tab, chips, half, c):
    return head_of(tab, me[0] ^ (half * chips + c))


def pack(me, tab, chips, source, mine, other):
    rows = source.shape[0]
    for half, out in ((0, mine), (1, other)):
        for c in range(chips):
            col = columns(jnp.maximum(head_at(me, tab, chips, half, c), 0))
            out[c * rows : (c + 1) * rows] = source[:, col]


def squares(ref):
    total = None
    for i in range(ref.shape[1] // HD):
        x = ref[:, tile(i)].astype(F32)
        total = x * x if total is None else total + x * x
    return total


def first_kernel(tab, chips, me, q_hbm, k_hbm, t_hbm, v_hbm, tv_hbm, mine, other, sums, q, k, t, v, sems):
    tokens = v_hbm.shape[0]
    copies = []
    pairs = [(v_hbm, v.at[:tokens]), (tv_hbm, v.at[tokens:]), (k_hbm, k), (q_hbm, q), (t_hbm, t)]
    for i, (a, b) in enumerate(pairs):
        copies.append(pltpu.make_async_copy(a, b, sems.at[i]))
        copies[-1].start()
    copies[0].wait()
    copies[1].wait()
    pack(me, tab, chips, v, mine, other)
    for copy in copies[2:]:
        copy.wait()
    parts = [squares(q), squares(k), squares(t)]
    rest = sums.shape[1] - sum(p.shape[0] for p in parts)
    if rest:
        parts.append(jnp.zeros((rest, HD), F32))
    sums[...] = rows_to_row(jnp.concatenate(parts, axis=0))


def merge_kernel(chips, mine, other, *outs):
    rows = mine.shape[0] // chips
    for c, out in enumerate(outs):
        out[:rows] = mine[c * rows : (c + 1) * rows]
        out[rows:] = other[c * rows : (c + 1) * rows]


def send_k_kernel(tab, width, count, chips, me, *refs):
    sums, (k, tk, gain, mine, other, scales, normed) = refs[:count], refs[count:]
    tokens, texts = k.shape[0], tk.shape[0]
    scale = lax.rsqrt(total_of(sums) * (1.0 / width) + EPS)
    scales[...] = scale
    cols = row_to_columns(scale[:, tokens:])
    for i in range(k.shape[1] // HD):
        g = gain[:, tile(i)]
        normed[:tokens, tile(i)] = (k[:, tile(i)].astype(F32) * cols[:tokens] * g).astype(BF)
        normed[tokens:, tile(i)] = (
            tk[:, tile(i)].astype(F32) * cols[tokens : tokens + texts] * g
        ).astype(BF)
    pack(me, tab, chips, normed, mine, other)


def send_q_kernel(tab, chips, me, vid, scales, q, gain, cot, mine, other, both):
    tokens = q.shape[0]
    cols = row_to_columns(scales[:, :tokens])
    row = me[0] * tokens + lax.broadcasted_iota(jnp.int32, (tokens, HD), 0)
    live = row < vid[0]
    for i in range(q.shape[1] // HD):
        g = gain[:, tile(i)]
        both[:tokens, tile(i)] = (q[:, tile(i)].astype(F32) * cols * g).astype(BF)
        both[tokens:, tile(i)] = jnp.where(live, cot[:, tile(i)].astype(F32), 0.0).astype(BF)
    pack(me, tab, chips, both, mine, other)


def places(members, tokens, texts, source):
    text_at = pl.ds(pl.multiple_of(source * texts, texts), texts)
    video_at = pl.ds(pl.multiple_of(members * texts + source * tokens, texts), tokens)
    return text_at, video_at


def assemble_kernel(chips, texts, me, *refs):
    pieces_v, pieces_k = refs[:chips], refs[chips : 2 * chips]
    k, v, kt, vt = refs[2 * chips :]
    span = pieces_v[0].shape[0] // 2
    tokens = span - texts
    for pieces, whole in ((pieces_k, k), (pieces_v, v)):
        for c in range(chips):
            for half in (0, 1):
                source = me[0] ^ (half * chips + c)
                text_at, video_at = places(2 * chips, tokens, texts, source)
                whole[text_at] = pieces[c][half * span + tokens : (half + 1) * span]
                whole[video_at] = pieces[c][half * span : half * span + tokens]
    for whole, turned in ((k, kt), (v, vt)):
        step = 256
        for start in range(0, whole.shape[0], step):
            turned[:, start : start + step] = whole[start : start + step, :].T


def attention_kernel(tab, spec, me, vid, txt, *refs):
    chips, tokens, texts, c, first, last, step = spec
    refs = list(refs)
    take = lambda count: [refs.pop(0) for _ in range(count)]
    (query,) = take(1)
    k, v, kt, vt = take(4)
    if not first:
        dk_in, dv_in, gain_in = take(3)
    (out,) = take(1)
    dk, dv, gains = take(3)
    if last:
        (dots,) = take(1)
    scores, weights, top, totals, turned_out, turned_dq = take(6)
    scale = HD ** (-0.5)
    span = 2 * chips * texts
    rows = k.shape[0]

    if first:
        dk[...] = jnp.zeros_like(dk)
        dv[...] = jnp.zeros_like(dv)
        gains[...] = jnp.zeros_like(gains)
    else:
        dk[...] = dk_in[...]
        dv[...] = dv_in[...]
        gains[...] = gain_in[...]

    blocks = span // step + (vid[0] + step - 1) // step

    def over_blocks(visit):
        def body(b, unused):
            start = pl.multiple_of(b * step, step)
            limit = jnp.where(start < span, txt[0] - start, vid[0] - (start - span))
            visit(pl.ds(start, step), limit)
            return unused

        lax.fori_loop(0, blocks, body, 0)

    def piece(half, unused):
        source = me[0] ^ (half * chips + c)
        active = jnp.logical_and(head_of(tab, me[0]) >= 0, source * tokens < vid[0])
        q_at = pl.ds(pl.multiple_of(half * 2 * tokens, tokens), tokens)
        grad_at = pl.ds(pl.multiple_of(half * 2 * tokens + tokens, tokens), tokens)

        @pl.when(jnp.logical_not(active))
        def _():
            out[q_at] = jnp.zeros((tokens, HD), BF)
            out[grad_at] = jnp.zeros((tokens, HD), BF)

        @pl.when(active)
        def _():
            q = query[q_at]
            grad = query[grad_at]
            top[...] = jnp.full_like(top, NEG)
            totals[...] = jnp.zeros_like(totals)
            turned_out[...] = jnp.zeros_like(turned_out)
            turned_dq[...] = jnp.zeros_like(turned_dq)

            def scan_scores(at, limit):
                s = nt(k[at], q)
                live = lax.broadcasted_iota(jnp.int32, s.shape, 0) < limit
                s = jnp.where(live, s, NEG)
                scores[at] = s
                top[...] = jnp.maximum(
                    top[...], jnp.max(s.reshape(step // 8, 8, tokens), axis=0)
                )

            over_blocks(scan_scores)
            highest = jnp.max(top[...], axis=0, keepdims=True) * (scale * LOG2E)

            def scan_weights(at, limit):
                p = jnp.exp2(scores[at] * (scale * LOG2E) - highest)
                totals[...] += jnp.sum(p.reshape(step // 8, 8, tokens), axis=0)
                low = p.astype(BF)
                weights[at] = low
                turned_out[...] += nn(vt[:, at], low)

            over_blocks(scan_weights)
            inverse = 1.0 / jnp.sum(totals[...], axis=0, keepdims=True)
            attention = turned_out[...] * inverse
            turned_grad = grad.astype(F32).T
            inner = jnp.sum(attention * turned_grad, axis=0, keepdims=True)
            inv_cols = row_to_columns(inverse)
            low_grad = (grad.astype(F32) * inv_cols).astype(BF)
            low_q = (q.astype(F32) * (inv_cols * scale)).astype(BF)
            out[q_at] = attention.T.astype(BF)

            def scan_grads(at, limit):
                p = weights[at]
                dp = nt(v[at], grad)
                ds = p * (dp - inner).astype(BF)
                dv[at] += nn(p, low_grad)
                dk[at] += nn(ds, low_q)
                turned_dq[...] += nn(kt[:, at], ds)

            over_blocks(scan_grads)
            dq = (turned_dq[...] * (inverse * scale)).T
            out[grad_at] = dq.astype(BF)
            part = dq * q.astype(F32)
            gains[...] += jnp.sum(part.reshape(tokens // 8, 8, HD), axis=0)

        return unused

    lax.fori_loop(0, 2, piece, 0)

    if last:
        for start in range(0, rows, step):
            at = slice(start, start + step)
            part = dk[at] * k[at].astype(F32)
            dots[:, at] = rows_to_row(part)
            gains_k = jnp.sum(part.reshape(step // 8, 8, HD), axis=0)
            if start == 0:
                top[:, :HD] = gains_k
            else:
                top[:, :HD] += gains_k
        gq = jnp.sum(gains[...], axis=0, keepdims=True)
        gk = jnp.sum(top[:, :HD], axis=0, keepdims=True)
        gains[...] = jnp.concatenate([gq, gk, jnp.zeros((6, HD), F32)], axis=0)


def split_rows(lines, rest):
    block = jnp.concatenate(lines, axis=0)
    high = block.astype(BF).astype(F32)
    both = [high, block - high]
    if rest:
        both.append(jnp.zeros((rest, HD), F32))
    return jnp.concatenate(both, axis=0).astype(BF)


def pack_v_kernel(chips, texts, me, dv, gains, *outs):
    span = outs[0].shape[0] // 2 - 16
    tokens = span - texts
    lines = split_rows([gains[0:1], gains[1:2]], 12)
    for c in range(chips):
        for half in (0, 1):
            source = me[0] ^ (half * chips + c)
            text_at, video_at = places(2 * chips, tokens, texts, source)
            base = half * (span + 16)
            outs[c][base : base + tokens] = dv[video_at].astype(BF)
            outs[c][base + tokens : base + span] = dv[text_at].astype(BF)
            outs[c][base + span : base + span + 16] = lines


def pack_k_kernel(chips, texts, count, me, dk, *refs):
    sums, outs, dots = refs[:count], refs[count:-1], refs[-1]
    dots[...] = total_of(sums)
    keys = dk.shape[0]
    text_total = 2 * chips * texts
    tokens = (keys - text_total) // (2 * chips)
    text_lines = [dots[:, tile(i)] for i in range(text_total // HD)]
    for c in range(chips):
        span = outs[c].shape[0] // 2
        for half in (0, 1):
            source = me[0] ^ (half * chips + c)
            text_at, video_at = places(2 * chips, tokens, texts, source)
            base = half * span
            outs[c][base : base + tokens] = dk[video_at].astype(BF)
            outs[c][base + tokens : base + tokens + texts] = dk[text_at].astype(BF)
            lines = list(text_lines)
            for i in range(tokens // HD):
                start = pl.multiple_of(text_total + source * tokens + i * HD, HD)
                lines.append(dots[:, pl.ds(start, HD)])
            rest = span - tokens - texts - 2 * len(lines)
            outs[c][base + tokens + texts : base + span] = split_rows(lines, rest)


def split_kernel(chips, *refs):
    out = refs[chips]
    rows = out.shape[0] // chips
    for c in range(chips):
        out[c * rows : (c + 1) * rows] = refs[c][rows:]


def each_head(me, tab, chips, blocks, other, visit):
    rows = other.shape[0] // chips
    for half in (0, 1):
        for c in range(chips):
            head = head_at(me, tab, chips, half, c)

            @pl.when(head >= 0)
            def _():
                col = columns(jnp.maximum(head, 0))
                if half:
                    visit(col, other, c * rows)
                else:
                    visit(col, blocks[c], 0)


def gather_q_kernel(tab, chips, me, vid, *refs):
    blocks, other = refs[:chips], refs[chips]
    q, gain, out, dq, dots = refs[chips + 1 :]
    tokens = q.shape[0]
    row = me[0] * tokens + lax.broadcasted_iota(jnp.int32, (tokens, HD), 0)
    live = row < vid[0]

    def visit(col, ref, at):
        o = ref[at : at + tokens].astype(F32)
        out[:, col] = jnp.where(live, o, 0.0).astype(BF)
        dq[:, col] = ref[at + tokens : at + 2 * tokens]

    each_head(me, tab, chips, blocks, other, visit)
    total = None
    for i in range(q.shape[1] // HD):
        term = q[:, tile(i)].astype(F32) * (dq[:, tile(i)].astype(F32) * gain[:, tile(i)])
        total = term if total is None else total + term
    dots[...] = rows_to_row(total)


def total_of(refs):
    total = refs[0][...]
    for ref in refs[1:]:
        total = total + ref[...]
    return total


def finish_q_kernel(width, count, *refs):
    dots = total_of(refs[:count])
    scales, q, dq, gain, out = refs[count:]
    scale = scales[:, : q.shape[0]]
    cols = row_to_columns(scale)
    back = row_to_columns(dots * (scale * scale * scale) * (1.0 / width))
    for i in range(q.shape[1] // HD):
        scaled = dq[:, tile(i)].astype(F32) * gain[:, tile(i)]
        out[:, tile(i)] = (cols * scaled - q[:, tile(i)].astype(F32) * back).astype(BF)


def gather_v_kernel(tab, chips, me, *refs):
    blocks, other = refs[:chips], refs[chips]
    q_gain, k_gain, out, text_out, dq_gain, dk_gain = refs[chips + 1 :]
    tokens, texts = out.shape[0], text_out.shape[0]

    def visit(col, ref, at):
        out[:, col] = ref[at : at + tokens]
        text_out[:, col] = ref[at + tokens : at + tokens + texts]
        lines = ref[at + tokens + texts : at + tokens + texts + 16].astype(F32)
        dq_gain[:, col] = (lines[0:1] + lines[2:3]) / q_gain[:, col]
        dk_gain[:, col] = (lines[1:2] + lines[3:4]) / k_gain[:, col]

    each_head(me, tab, chips, blocks, other, visit)


def finish_k_kernel(tab, width, chips, me, *refs):
    blocks, other = refs[:chips], refs[chips]
    scales, k, tk, k_gain = refs[chips + 1 : chips + 5]
    out, text_out, dk, sums, text_cols = refs[chips + 5 :]
    tokens, texts = k.shape[0], tk.shape[0]
    text_lines = 2 * chips * texts // HD
    lines = text_lines + tokens // HD
    sums[...] = jnp.zeros_like(sums)

    def visit(col, ref, at):
        dk[:, col] = ref[at : at + tokens + texts]
        block = ref[at + tokens + texts : at + tokens + texts + 2 * lines].astype(F32)
        block = block[:lines] + block[lines:]
        sums[:lines] += block

    each_head(me, tab, chips, blocks, other, visit)
    for i in range(text_lines):
        text_cols[i * HD : (i + 1) * HD] = row_to_columns(sums[i : i + 1])
    scale = scales[:, tokens:]
    cols = row_to_columns(scale)
    text_at = pl.ds(pl.multiple_of(me[0] * texts, texts), texts)
    dots = [row_to_columns(sums[text_lines + i : text_lines + 1 + i]) for i in range(tokens // HD)]
    dots.append(text_cols[text_at])
    rows = tokens + texts
    back = jnp.concatenate(dots, axis=0) * (cols[:rows] * cols[:rows]) * (1.0 / width)
    for i in range(k.shape[1] // HD):
        scaled = dk[:, tile(i)].astype(F32) * k_gain[:, tile(i)]
        scaled = cols[:rows] * scaled
        out[:, tile(i)] = (scaled[:tokens] - k[:, tile(i)].astype(F32) * back[:tokens]).astype(BF)
        text_out[:, tile(i)] = (
            scaled[tokens:] - tk[:, tile(i)].astype(F32) * back[tokens:]
        ).astype(BF)


def local(q_raw, k_raw, values, text_k, text_v, q_gain, k_gain, cotangent, vid_len, txt_len):
    tokens, cols = q_raw.shape
    texts = text_k.shape[0]
    heads = cols // HD
    chips = lax.axis_size("ctx")
    members = 2 * chips
    parts = lax.axis_size("tp")
    width = cols * parts
    table = head_owners(members, chips, heads)
    span = tokens + texts
    keys = members * span
    text_total = members * texts
    pad = -(-(2 * tokens + texts) // HD) * HD
    extra = -(-2 * (text_total // HD + tokens // HD) // 16) * 16

    me = lax.axis_index(GROUP).astype(jnp.int32).reshape(1)
    tab = tuple(int(h) for h in table)
    qg = q_gain.reshape(1, cols)
    kg = k_gain.reshape(1, cols)

    def along(block, c, to_owner):
        if c == 0:
            return block
        pairs = [(s, s ^ c) for s in range(members) if table[s ^ c if to_owner else s] >= 0]
        return lax.ppermute(block, GROUP, pairs)

    def sibling(block):
        return lax.ppermute(block, "section", [(0, 1), (1, 0)])

    def shared(block):
        got = [block]
        for d in range(1, parts):
            got.append(lax.ppermute(block, "tp", [(s, s ^ d) for s in range(parts)]))
        return got

    far_first = far_chips(chips)
    chip_order = [0] + far_first

    def merged(mine, other):
        rows = mine.shape[0] // chips
        messages = call(
            functools.partial(merge_kernel, chips),
            [shaped((2 * rows, HD), BF)] * chips,
            [mine, sibling(other)],
        )
        got = {c: along(messages[c], c, True) for c in far_first}
        got[0] = messages[0]
        return [got[c] for c in range(chips)]

    mine_v, other_v, sums = call(
        functools.partial(first_kernel, tab, chips),
        [shaped((chips * span, HD), BF)] * 2 + [shaped((1, pad), F32)],
        [me, q_raw, k_raw, text_k, values, text_v],
        smem=1,
        scratch=[
            pltpu.VMEM((tokens, cols), BF),
            pltpu.VMEM((tokens, cols), BF),
            pltpu.VMEM((texts, cols), BF),
            pltpu.VMEM((span, cols), BF),
            pltpu.SemaphoreType.DMA((5,)),
        ],
        space=pl.BlockSpec(memory_space=pltpu.HBM),
    )
    sums = shared(sums)
    got_v = merged(mine_v, other_v)
    mine_k, other_k, scales = call(
        functools.partial(send_k_kernel, tab, width, parts, chips),
        [shaped((chips * span, HD), BF)] * 2 + [shaped((1, pad), F32)],
        [me, *sums, k_raw, text_k, kg],
        smem=1,
        scratch=[pltpu.VMEM((span, cols), BF)],
    )
    got_k = merged(mine_k, other_k)
    mine_q, other_q = call(
        functools.partial(send_q_kernel, tab, chips),
        [shaped((chips * 2 * tokens, HD), BF)] * 2,
        [me, vid_len, scales, q_raw, qg, cotangent],
        smem=2,
        scratch=[pltpu.VMEM((2 * tokens, cols), BF)],
    )
    got_q = merged(mine_q, other_q)

    whole = call(
        functools.partial(assemble_kernel, chips, texts),
        [shaped((keys, HD), BF)] * 2 + [shaped((HD, keys), BF)] * 2,
        [me, *got_v, *got_k],
        smem=1,
    )

    carry = ()
    back_q = {}
    step = 512
    for i, c in enumerate(chip_order):
        first, last = i == 0, i == chips - 1
        outs = [shaped((4 * tokens, HD), BF)]
        outs += [shaped((keys, HD), F32)] * 2 + [shaped((8, HD), F32)]
        if last:
            outs.append(shaped((1, keys), F32))
        ins = [me, vid_len, txt_len, got_q[c], *whole, *carry]
        result = call(
            functools.partial(attention_kernel, tab, (chips, tokens, texts, c, first, last, step)),
            outs,
            ins,
            smem=3,
            scratch=[
                pltpu.VMEM((keys, tokens), F32),
                pltpu.VMEM((keys, tokens), BF),
                pltpu.VMEM((8, tokens), F32),
                pltpu.VMEM((8, tokens), F32),
                pltpu.VMEM((HD, tokens), F32),
                pltpu.VMEM((HD, tokens), F32),
            ],
            flops=6 * 2 * 2 * tokens * keys * HD * 2,
            aliases={} if first else {8: 1, 9: 2, 10: 3},
        )
        back_q[c] = along(result[0], c, False)
        carry = result[1:4]
    dk_sum, dv_sum, gains = carry
    dv_parts = call(
        functools.partial(pack_v_kernel, chips, texts),
        [shaped((2 * (span + 16), HD), BF)] * chips,
        [me, dv_sum, gains],
        smem=1,
    )
    back_v = {c: along(dv_parts[c], c, False) for c in far_first + [0]}
    dots = shared(result[4])
    dk_parts = call(
        functools.partial(pack_k_kernel, chips, texts, parts),
        [shaped((2 * (span + extra), HD), BF)] * chips,
        [me, dk_sum, *dots],
        smem=1,
        scratch=[pltpu.VMEM((1, keys), F32)],
    )
    back_k = {c: along(dk_parts[c], c, False) for c in far_first + [0]}

    def mine_and_other(back):
        blocks = [back[c] for c in range(chips)]
        rows = blocks[0].shape[0] // 2
        (other,) = call(
            functools.partial(split_kernel, chips), [shaped((chips * rows, HD), BF)], blocks
        )
        return [*blocks, sibling(other)]

    attention_out, dq, dots_q = call(
        functools.partial(gather_q_kernel, tab, chips),
        [shaped((tokens, cols), BF)] * 2 + [shaped((1, tokens), F32)],
        [me, vid_len, *mine_and_other(back_q), q_raw, qg],
        smem=2,
    )
    (d_q_raw,) = call(
        functools.partial(finish_q_kernel, width, parts),
        [shaped((tokens, cols), BF)],
        [*shared(dots_q), scales, q_raw, dq, qg],
    )
    d_values, d_text_v, d_q_gain, d_k_gain = call(
        functools.partial(gather_v_kernel, tab, chips),
        [shaped((tokens, cols), BF), shaped((texts, cols), BF)] + [shaped((1, cols), F32)] * 2,
        [me, *mine_and_other(back_v), qg, kg],
        smem=1,
    )
    d_k_raw, d_text_k = call(
        functools.partial(finish_k_kernel, tab, width, chips),
        [shaped((tokens, cols), BF), shaped((texts, cols), BF)],
        [me, *mine_and_other(back_k), scales, k_raw, text_k, kg],
        smem=1,
        scratch=[
            pltpu.VMEM((span, cols), BF),
            pltpu.VMEM((extra, HD), F32),
            pltpu.VMEM((text_total, HD), F32),
        ],
    )
    return (
        attention_out,
        d_q_raw,
        d_k_raw,
        d_values,
        d_text_k,
        d_text_v,
        d_q_gain.reshape(cols),
        d_k_gain.reshape(cols),
    )


def far_chips(chips):
    return sorted(range(1, chips), key=lambda c: (-c.bit_length(), c))


def solution(mesh):
    rows = P(GROUP, "tp")
    return jax.shard_map(
        local,
        mesh=mesh,
        in_specs=(rows,) * 5 + (P("tp"), P("tp"), rows, P(), P()),
        out_specs=(rows,) * 6 + (P("tp"), P("tp")),
        check_vma=False,
    )
```

```python
import functools

import jax
import jax.numpy as jnp
import numpy as np
from jax import lax
from jax.experimental import pallas as pl
from jax.experimental.pallas import tpu as pltpu
from jax.sharding import PartitionSpec as P


HD = 128
EPS = 1e-06
NEG = -1e30
LOG2E = 1.4426950408889634
GROUP = ("section", "ctx")
BF = jnp.bfloat16
F32 = jnp.float32


VM = pl.BlockSpec(memory_space=pltpu.VMEM)
SM = pl.BlockSpec(memory_space=pltpu.SMEM)


def head_owners(members, chips, heads):
    order = sorted(range(members), key=lambda d: (abs(2 * (d % chips) - (chips - 1)), d))
    table = np.full((members,), -1, np.int32)
    for head, device in enumerate(order[:heads]):
        table[device] = head
    return table


def columns(head):
    return pl.ds(pl.multiple_of(head * HD, HD), HD)


def tile(i):
    return slice(i * HD, (i + 1) * HD)


def row_to_columns(row):
    return jnp.broadcast_to(row, (HD, row.shape[1])).T


def rows_to_row(block):
    return jnp.sum(block.T, axis=0, keepdims=True)


def nt(a, b):
    return lax.dot_general(a, b, (((1,), (1,)), ((), ())), preferred_element_type=F32)


def nn(a, b):
    return jnp.dot(a, b, preferred_element_type=F32)


def call(kernel, outs, ins, smem=0, scratch=(), flops=0, aliases=None, vmem=24, space=None):
    nbytes = sum(int(np.prod(o.shape)) * o.dtype.itemsize for o in list(outs) + list(ins)[smem:])
    big = VM if space is None else space
    return pl.pallas_call(
        kernel,
        out_shape=tuple(jax.ShapeDtypeStruct(o.shape, o.dtype) for o in outs),
        in_specs=[SM] * smem + [big] * (len(ins) - smem),
        out_specs=tuple(VM for _ in outs),
        scratch_shapes=list(scratch),
        input_output_aliases=aliases or {},
        compiler_params=pltpu.CompilerParams(vmem_limit_bytes=vmem << 20),
        cost_estimate=pl.CostEstimate(flops=flops, bytes_accessed=nbytes, transcendentals=0),
    )(*ins)


def shaped(shape, dtype):
    return jax.ShapeDtypeStruct(shape, dtype)


def head_of(tab, device):
    head = jnp.int32(-1)
    for d, h in enumerate(tab):
        if h >= 0:
            head = jnp.where(device == d, jnp.int32(h), head)
    return head


def head_at(me, tab, chips, half, c):
    return head_of(tab, me[0] ^ (half * chips + c))


def pack(me, tab, chips, source, mine, other):
    rows = source.shape[0]
    for half, out in ((0, mine), (1, other)):
        for c in range(chips):
            col = columns(jnp.maximum(head_at(me, tab, chips, half, c), 0))
            out[c * rows : (c + 1) * rows] = source[:, col]


def squares(ref):
    total = None
    for i in range(ref.shape[1] // HD):
        x = ref[:, tile(i)].astype(F32)
        total = x * x if total is None else total + x * x
    return total


def first_kernel(tab, chips, me, q_hbm, k_hbm, t_hbm, v_hbm, tv_hbm, mine, other, sums, q, k, t, v, sems):
    tokens = v_hbm.shape[0]
    copies = []
    pairs = [(v_hbm, v.at[:tokens]), (tv_hbm, v.at[tokens:]), (k_hbm, k), (q_hbm, q), (t_hbm, t)]
    for i, (a, b) in enumerate(pairs):
        copies.append(pltpu.make_async_copy(a, b, sems.at[i]))
        copies[-1].start()
    copies[0].wait()
    copies[1].wait()
    pack(me, tab, chips, v, mine, other)
    for copy in copies[2:]:
        copy.wait()
    parts = [squares(q), squares(k), squares(t)]
    rest = sums.shape[1] - sum(p.shape[0] for p in parts)
    if rest:
        parts.append(jnp.zeros((rest, HD), F32))
    sums[...] = rows_to_row(jnp.concatenate(parts, axis=0))


def merge_kernel(chips, mine, other, *outs):
    rows = mine.shape[0] // chips
    for c, out in enumerate(outs):
        out[:rows] = mine[c * rows : (c + 1) * rows]
        out[rows:] = other[c * rows : (c + 1) * rows]


def send_k_kernel(tab, width, count, chips, me, *refs):
    sums, (k, tk, gain, mine, other, scales, normed) = refs[:count], refs[count:]
    tokens, texts = k.shape[0], tk.shape[0]
    scale = lax.rsqrt(total_of(sums) * (1.0 / width) + EPS)
    scales[...] = scale
    cols = row_to_columns(scale[:, tokens:])
    for i in range(k.shape[1] // HD):
        g = gain[:, tile(i)]
        normed[:tokens, tile(i)] = (k[:, tile(i)].astype(F32) * cols[:tokens] * g).astype(BF)
        normed[tokens:, tile(i)] = (
            tk[:, tile(i)].astype(F32) * cols[tokens : tokens + texts] * g
        ).astype(BF)
    pack(me, tab, chips, normed, mine, other)


def send_q_kernel(tab, chips, me, vid, scales, q, gain, cot, mine, other, both):
    tokens = q.shape[0]
    cols = row_to_columns(scales[:, :tokens])
    row = me[0] * tokens + lax.broadcasted_iota(jnp.int32, (tokens, HD), 0)
    live = row < vid[0]
    for i in range(q.shape[1] // HD):
        g = gain[:, tile(i)]
        both[:tokens, tile(i)] = (q[:, tile(i)].astype(F32) * cols * g).astype(BF)
        both[tokens:, tile(i)] = jnp.where(live, cot[:, tile(i)].astype(F32), 0.0).astype(BF)
    pack(me, tab, chips, both, mine, other)


def places(members, tokens, texts, source):
    text_at = pl.ds(pl.multiple_of(source * texts, texts), texts)
    video_at = pl.ds(pl.multiple_of(members * texts + source * tokens, texts), tokens)
    return text_at, video_at


def assemble_kernel(chips, texts, me, *refs):
    pieces_v, pieces_k = refs[:chips], refs[chips : 2 * chips]
    k, v, kt, vt = refs[2 * chips :]
    span = pieces_v[0].shape[0] // 2
    tokens = span - texts
    for pieces, whole in ((pieces_k, k), (pieces_v, v)):
        for c in range(chips):
            for half in (0, 1):
                source = me[0] ^ (half * chips + c)
                text_at, video_at = places(2 * chips, tokens, texts, source)
                whole[text_at] = pieces[c][half * span + tokens : (half + 1) * span]
                whole[video_at] = pieces[c][half * span : half * span + tokens]
    for whole, turned in ((k, kt), (v, vt)):
        step = 256
        for start in range(0, whole.shape[0], step):
            turned[:, start : start + step] = whole[start : start + step, :].T


def attention_kernel(tab, spec, me, vid, txt, query, k, v, kt, vt, *refs):
    chips, tokens, texts, c, step = spec
    out, dk, dv, gains, scores, weights, top, totals, turned_out, turned_dq = refs
    scale = HD ** (-0.5)
    span = 2 * chips * texts
    rows = k.shape[0]
    videos = rows - span
    blocks = [slice(start, start + step) for start in range(0, rows, step)]
    low_text, low_video = span * 3 // 4, span + videos // 2

    gains[...] = jnp.zeros_like(gains)

    def masked(s, start):
        parts = []
        for begin, end, limit in (
            (0, low_text, None),
            (low_text, span, txt[0]),
            (span, low_video, None),
            (low_video, rows, span + vid[0]),
        ):
            begin, end = max(begin, start), min(end, start + step)
            if begin >= end:
                continue
            part = s[begin - start : end - start]
            if limit is not None:
                row = lax.broadcasted_iota(jnp.int32, part.shape, 0)
                part = jnp.where(row < limit - begin, part, NEG)
            parts.append(part)
        return parts[0] if len(parts) == 1 else jnp.concatenate(parts, axis=0)

    def piece(half, unused):
        source = me[0] ^ (half * chips + c)
        active = jnp.logical_and(head_of(tab, me[0]) >= 0, source * tokens < vid[0])
        q_at = pl.ds(pl.multiple_of(half * 2 * tokens, tokens), tokens)
        grad_at = pl.ds(pl.multiple_of(half * 2 * tokens + tokens, tokens), tokens)

        @pl.when(jnp.logical_not(active))
        def _():
            out[q_at] = jnp.zeros((tokens, HD), BF)
            out[grad_at] = jnp.zeros((tokens, HD), BF)

            @pl.when(half == 0)
            def _():
                dk[...] = jnp.zeros_like(dk)
                dv[...] = jnp.zeros_like(dv)

        def work(add):
            q = query[q_at]
            grad = query[grad_at]
            for i, at in enumerate(blocks):
                s = masked(nt(k[at], q), at.start)
                scores[at] = s
                most = jnp.max(s.reshape(step // 8, 8, tokens), axis=0)
                top[...] = most if i == 0 else jnp.maximum(top[...], most)
            highest = jnp.max(top[...], axis=0, keepdims=True) * (scale * LOG2E)
            for i, at in enumerate(blocks):
                p = jnp.exp2(scores[at] * (scale * LOG2E) - highest)
                part = jnp.sum(p.reshape(step // 8, 8, tokens), axis=0)
                low = p.astype(BF)
                weights[at] = low
                o = nn(vt[:, at], low)
                totals[...] = part if i == 0 else totals[...] + part
                turned_out[...] = o if i == 0 else turned_out[...] + o
            inverse = 1.0 / jnp.sum(totals[...], axis=0, keepdims=True)
            attention = turned_out[...] * inverse
            turned_grad = grad.astype(F32).T
            inner = jnp.sum(attention * turned_grad, axis=0, keepdims=True)
            inv_cols = row_to_columns(inverse)
            low_grad = (grad.astype(F32) * inv_cols).astype(BF)
            low_q = (q.astype(F32) * (inv_cols * scale)).astype(BF)
            out[q_at] = attention.T.astype(BF)
            for i, at in enumerate(blocks):
                p = weights[at]
                dp = nt(v[at], grad)
                ds = p * (dp - inner).astype(BF)
                dv_part, dk_part = nn(p, low_grad), nn(ds, low_q)
                dv[at] = jnp.where(add, dv[at], 0.0) + dv_part
                dk[at] = jnp.where(add, dk[at], 0.0) + dk_part
                dq = nn(kt[:, at], ds)
                turned_dq[...] = dq if i == 0 else turned_dq[...] + dq
            dq = (turned_dq[...] * (inverse * scale)).T
            out[grad_at] = dq.astype(BF)
            part = dq * q.astype(F32)
            gains[...] += jnp.sum(part.reshape(tokens // 8, 8, HD), axis=0)

        @pl.when(active)
        def _():
            work(half > 0)

        return unused

    lax.fori_loop(0, 2, piece, 0)


def attention_scratch(keys, tokens):
    return [
        pltpu.VMEM((keys, tokens), F32),
        pltpu.VMEM((keys, tokens), BF),
        pltpu.VMEM((8, tokens), F32),
        pltpu.VMEM((8, tokens), F32),
        pltpu.VMEM((HD, tokens), F32),
        pltpu.VMEM((HD, tokens), F32),
    ]


def split_rows(lines, rest):
    block = jnp.concatenate(lines, axis=0)
    high = block.astype(BF).astype(F32)
    both = [high, block - high]
    if rest:
        both.append(jnp.zeros((rest, HD), F32))
    return jnp.concatenate(both, axis=0).astype(BF)


def pack_v_kernel(chips, texts, me, k, *refs):
    dks, dvs, gains = refs[:chips], refs[chips : 2 * chips], refs[2 * chips : 3 * chips]
    outs, dk, dots, dv = refs[3 * chips : 4 * chips], refs[4 * chips], refs[4 * chips + 1], refs[-1]
    span = outs[0].shape[0] // 2 - 16
    tokens = span - texts
    rows, step = k.shape[0], 512
    gk = jnp.zeros((8, HD), F32)
    for start in range(0, rows, step):
        at = slice(start, min(start + step, rows))
        total = functools.reduce(lambda a, b: a + b, [ref[at] for ref in dks])
        dk[at] = total
        part = total * k[at].astype(F32)
        dots[:, at] = rows_to_row(part)
        gk = gk + jnp.sum(part.reshape(part.shape[0] // 8, 8, HD), axis=0)
        dv[at] = functools.reduce(lambda a, b: a + b, [ref[at] for ref in dvs]).astype(BF)
    gq = functools.reduce(lambda a, b: a + b, [ref[...] for ref in gains])
    gq = jnp.sum(gq, axis=0, keepdims=True)
    lines = split_rows([gq, jnp.sum(gk, axis=0, keepdims=True)], 12)
    for c in range(chips):
        for half in (0, 1):
            source = me[0] ^ (half * chips + c)
            text_at, video_at = places(2 * chips, tokens, texts, source)
            base = half * (span + 16)
            outs[c][base : base + tokens] = dv[video_at]
            outs[c][base + tokens : base + span] = dv[text_at]
            outs[c][base + span : base + span + 16] = lines


def pack_k_kernel(chips, texts, count, me, dk, *refs):
    sums, outs, dots = refs[:count], refs[count:-1], refs[-1]
    dots[...] = total_of(sums)
    keys = dk.shape[0]
    text_total = 2 * chips * texts
    tokens = (keys - text_total) // (2 * chips)
    text_lines = [dots[:, tile(i)] for i in range(text_total // HD)]
    for c in range(chips):
        span = outs[c].shape[0] // 2
        for half in (0, 1):
            source = me[0] ^ (half * chips + c)
            text_at, video_at = places(2 * chips, tokens, texts, source)
            base = half * span
            outs[c][base : base + tokens] = dk[video_at].astype(BF)
            outs[c][base + tokens : base + tokens + texts] = dk[text_at].astype(BF)
            lines = list(text_lines)
            for i in range(tokens // HD):
                start = pl.multiple_of(text_total + source * tokens + i * HD, HD)
                lines.append(dots[:, pl.ds(start, HD)])
            rest = span - tokens - texts - 2 * len(lines)
            outs[c][base + tokens + texts : base + span] = split_rows(lines, rest)


def split_kernel(chips, *refs):
    out = refs[chips]
    rows = out.shape[0] // chips
    for c in range(chips):
        out[c * rows : (c + 1) * rows] = refs[c][rows:]


def each_head(me, tab, chips, blocks, other, visit):
    rows = other.shape[0] // chips
    for half in (0, 1):
        for c in range(chips):
            head = head_at(me, tab, chips, half, c)

            @pl.when(head >= 0)
            def _():
                col = columns(jnp.maximum(head, 0))
                if half:
                    visit(col, other, c * rows)
                else:
                    visit(col, blocks[c], 0)


def gather_q_kernel(tab, chips, me, vid, *refs):
    blocks, other = refs[:chips], refs[chips]
    q, gain, out, dq, dots = refs[chips + 1 :]
    tokens = q.shape[0]
    row = me[0] * tokens + lax.broadcasted_iota(jnp.int32, (tokens, HD), 0)
    live = row < vid[0]

    def visit(col, ref, at):
        o = ref[at : at + tokens].astype(F32)
        out[:, col] = jnp.where(live, o, 0.0).astype(BF)
        dq[:, col] = ref[at + tokens : at + 2 * tokens]

    each_head(me, tab, chips, blocks, other, visit)
    total = None
    for i in range(q.shape[1] // HD):
        term = q[:, tile(i)].astype(F32) * (dq[:, tile(i)].astype(F32) * gain[:, tile(i)])
        total = term if total is None else total + term
    dots[...] = rows_to_row(total)


def total_of(refs):
    total = refs[0][...]
    for ref in refs[1:]:
        total = total + ref[...]
    return total


def finish_q_kernel(width, count, *refs):
    dots = total_of(refs[:count])
    scales, q, dq, gain, out = refs[count:]
    scale = scales[:, : q.shape[0]]
    cols = row_to_columns(scale)
    back = row_to_columns(dots * (scale * scale * scale) * (1.0 / width))
    for i in range(q.shape[1] // HD):
        scaled = dq[:, tile(i)].astype(F32) * gain[:, tile(i)]
        out[:, tile(i)] = (cols * scaled - q[:, tile(i)].astype(F32) * back).astype(BF)


def gather_v_kernel(tab, chips, me, *refs):
    blocks, other = refs[:chips], refs[chips]
    q_gain, k_gain, out, text_out, dq_gain, dk_gain = refs[chips + 1 :]
    tokens, texts = out.shape[0], text_out.shape[0]

    def visit(col, ref, at):
        out[:, col] = ref[at : at + tokens]
        text_out[:, col] = ref[at + tokens : at + tokens + texts]
        lines = ref[at + tokens + texts : at + tokens + texts + 16].astype(F32)
        dq_gain[:, col] = (lines[0:1] + lines[2:3]) / q_gain[:, col]
        dk_gain[:, col] = (lines[1:2] + lines[3:4]) / k_gain[:, col]

    each_head(me, tab, chips, blocks, other, visit)


def finish_k_kernel(tab, width, chips, me, *refs):
    blocks, other = refs[:chips], refs[chips]
    scales, k, tk, k_gain = refs[chips + 1 : chips + 5]
    out, text_out, dk, sums, text_cols = refs[chips + 5 :]
    tokens, texts = k.shape[0], tk.shape[0]
    text_lines = 2 * chips * texts // HD
    lines = text_lines + tokens // HD
    sums[...] = jnp.zeros_like(sums)

    def visit(col, ref, at):
        dk[:, col] = ref[at : at + tokens + texts]
        block = ref[at + tokens + texts : at + tokens + texts + 2 * lines].astype(F32)
        block = block[:lines] + block[lines:]
        sums[:lines] += block

    each_head(me, tab, chips, blocks, other, visit)
    for i in range(text_lines):
        text_cols[i * HD : (i + 1) * HD] = row_to_columns(sums[i : i + 1])
    scale = scales[:, tokens:]
    cols = row_to_columns(scale)
    text_at = pl.ds(pl.multiple_of(me[0] * texts, texts), texts)
    dots = [row_to_columns(sums[text_lines + i : text_lines + 1 + i]) for i in range(tokens // HD)]
    dots.append(text_cols[text_at])
    rows = tokens + texts
    back = jnp.concatenate(dots, axis=0) * (cols[:rows] * cols[:rows]) * (1.0 / width)
    for i in range(k.shape[1] // HD):
        scaled = dk[:, tile(i)].astype(F32) * k_gain[:, tile(i)]
        scaled = cols[:rows] * scaled
        out[:, tile(i)] = (scaled[:tokens] - k[:, tile(i)].astype(F32) * back[:tokens]).astype(BF)
        text_out[:, tile(i)] = (
            scaled[tokens:] - tk[:, tile(i)].astype(F32) * back[tokens:]
        ).astype(BF)


def local(q_raw, k_raw, values, text_k, text_v, q_gain, k_gain, cotangent, vid_len, txt_len):
    tokens, cols = q_raw.shape
    texts = text_k.shape[0]
    heads = cols // HD
    chips = lax.axis_size("ctx")
    members = 2 * chips
    parts = lax.axis_size("tp")
    width = cols * parts
    table = head_owners(members, chips, heads)
    span = tokens + texts
    keys = members * span
    text_total = members * texts
    pad = -(-(2 * tokens + texts) // HD) * HD
    extra = -(-2 * (text_total // HD + tokens // HD) // 16) * 16

    me = lax.axis_index(GROUP).astype(jnp.int32).reshape(1)
    tab = tuple(int(h) for h in table)
    qg = q_gain.reshape(1, cols)
    kg = k_gain.reshape(1, cols)

    def along(block, c, to_owner):
        if c == 0:
            return block
        pairs = [(s, s ^ c) for s in range(members) if table[s ^ c if to_owner else s] >= 0]
        return lax.ppermute(block, GROUP, pairs)

    def sibling(block):
        return lax.ppermute(block, "section", [(0, 1), (1, 0)])

    def shared(block):
        got = [block]
        for d in range(1, parts):
            got.append(lax.ppermute(block, "tp", [(s, s ^ d) for s in range(parts)]))
        return got

    far_first = far_chips(chips)
    chip_order = [0] + far_first

    def merged(mine, other):
        rows = mine.shape[0] // chips
        messages = call(
            functools.partial(merge_kernel, chips),
            [shaped((2 * rows, HD), BF)] * chips,
            [mine, sibling(other)],
        )
        got = {c: along(messages[c], c, True) for c in far_first}
        got[0] = messages[0]
        return [got[c] for c in range(chips)]

    mine_v, other_v, sums = call(
        functools.partial(first_kernel, tab, chips),
        [shaped((chips * span, HD), BF)] * 2 + [shaped((1, pad), F32)],
        [me, q_raw, k_raw, text_k, values, text_v],
        smem=1,
        scratch=[
            pltpu.VMEM((tokens, cols), BF),
            pltpu.VMEM((tokens, cols), BF),
            pltpu.VMEM((texts, cols), BF),
            pltpu.VMEM((span, cols), BF),
            pltpu.SemaphoreType.DMA((5,)),
        ],
        space=pl.BlockSpec(memory_space=pltpu.HBM),
        vmem=60,
    )
    sums = shared(sums)
    got_v = merged(mine_v, other_v)
    mine_k, other_k, scales = call(
        functools.partial(send_k_kernel, tab, width, parts, chips),
        [shaped((chips * span, HD), BF)] * 2 + [shaped((1, pad), F32)],
        [me, *sums, k_raw, text_k, kg],
        smem=1,
        scratch=[pltpu.VMEM((span, cols), BF)],
    )
    got_k = merged(mine_k, other_k)
    mine_q, other_q = call(
        functools.partial(send_q_kernel, tab, chips),
        [shaped((chips * 2 * tokens, HD), BF)] * 2,
        [me, vid_len, scales, q_raw, qg, cotangent],
        smem=2,
        scratch=[pltpu.VMEM((2 * tokens, cols), BF)],
    )
    got_q = merged(mine_q, other_q)

    whole = call(
        functools.partial(assemble_kernel, chips, texts),
        [shaped((keys, HD), BF)] * 2 + [shaped((HD, keys), BF)] * 2,
        [me, *got_v, *got_k],
        smem=1,
    )

    back_q = {}
    dk_calls, dv_calls, gain_calls = [], [], []
    step = max(d for d in range(256, 1281, 128) if keys % d == 0)
    for c in chip_order:
        block, dk_call, dv_call, gain_call = call(
            functools.partial(attention_kernel, tab, (chips, tokens, texts, c, step)),
            [shaped((4 * tokens, HD), BF)]
            + [shaped((keys, HD), F32)] * 2
            + [shaped((8, HD), F32)],
            [me, vid_len, txt_len, got_q[c], *whole],
            smem=3,
            scratch=attention_scratch(keys, tokens),
            flops=6 * 2 * 2 * tokens * keys * HD * 2,
        )
        back_q[c] = along(block, c, False)
        dk_calls.append(dk_call)
        dv_calls.append(dv_call)
        gain_calls.append(gain_call)
    *dv_parts, dk_sum, dots = call(
        functools.partial(pack_v_kernel, chips, texts),
        [shaped((2 * (span + 16), HD), BF)] * chips
        + [shaped((keys, HD), F32), shaped((1, keys), F32)],
        [me, whole[0], *dk_calls, *dv_calls, *gain_calls],
        smem=1,
        scratch=[pltpu.VMEM((keys, HD), BF)],
    )
    back_v = {c: along(dv_parts[c], c, False) for c in far_first + [0]}
    dots = shared(dots)
    dk_parts = call(
        functools.partial(pack_k_kernel, chips, texts, parts),
        [shaped((2 * (span + extra), HD), BF)] * chips,
        [me, dk_sum, *dots],
        smem=1,
        scratch=[pltpu.VMEM((1, keys), F32)],
    )
    back_k = {c: along(dk_parts[c], c, False) for c in far_first + [0]}

    def mine_and_other(back):
        blocks = [back[c] for c in range(chips)]
        rows = blocks[0].shape[0] // 2
        (other,) = call(
            functools.partial(split_kernel, chips), [shaped((chips * rows, HD), BF)], blocks
        )
        return [*blocks, sibling(other)]

    attention_out, dq, dots_q = call(
        functools.partial(gather_q_kernel, tab, chips),
        [shaped((tokens, cols), BF)] * 2 + [shaped((1, tokens), F32)],
        [me, vid_len, *mine_and_other(back_q), q_raw, qg],
        smem=2,
    )
    (d_q_raw,) = call(
        functools.partial(finish_q_kernel, width, parts),
        [shaped((tokens, cols), BF)],
        [*shared(dots_q), scales, q_raw, dq, qg],
    )
    d_values, d_text_v, d_q_gain, d_k_gain = call(
        functools.partial(gather_v_kernel, tab, chips),
        [shaped((tokens, cols), BF), shaped((texts, cols), BF)] + [shaped((1, cols), F32)] * 2,
        [me, *mine_and_other(back_v), qg, kg],
        smem=1,
    )
    d_k_raw, d_text_k = call(
        functools.partial(finish_k_kernel, tab, width, chips),
        [shaped((tokens, cols), BF), shaped((texts, cols), BF)],
        [me, *mine_and_other(back_k), scales, k_raw, text_k, kg],
        smem=1,
        scratch=[
            pltpu.VMEM((span, cols), BF),
            pltpu.VMEM((extra, HD), F32),
            pltpu.VMEM((text_total, HD), F32),
        ],
    )
    return (
        attention_out,
        d_q_raw,
        d_k_raw,
        d_values,
        d_text_k,
        d_text_v,
        d_q_gain.reshape(cols),
        d_k_gain.reshape(cols),
    )


def far_chips(chips):
    return sorted(range(1, chips), key=lambda c: (-c.bit_length(), c))


def solution(mesh):
    rows = P(GROUP, "tp")
    return jax.shard_map(
        local,
        mesh=mesh,
        in_specs=(rows,) * 5 + (P("tp"), P("tp"), rows, P(), P()),
        out_specs=(rows,) * 6 + (P("tp"), P("tp")),
        check_vma=False,
    )
```

```python
import functools

import jax
import jax.numpy as jnp
import numpy as np
from jax import lax
from jax.experimental import pallas as pl
from jax.experimental.pallas import tpu as pltpu
from jax.sharding import PartitionSpec as P


HD = 128
EPS = 1e-06
NEG = -1e30
LOG2E = 1.4426950408889634
GROUP = ("section", "ctx")
BF = jnp.bfloat16
F32 = jnp.float32


VM = pl.BlockSpec(memory_space=pltpu.VMEM)
SM = pl.BlockSpec(memory_space=pltpu.SMEM)


def head_owners(members, chips, heads):
    order = sorted(range(members), key=lambda d: (abs(2 * (d % chips) - (chips - 1)), d))
    table = np.full((members,), -1, np.int32)
    for head, device in enumerate(order[:heads]):
        table[device] = head
    return table


def columns(head):
    return pl.ds(pl.multiple_of(head * HD, HD), HD)


def tile(i):
    return slice(i * HD, (i + 1) * HD)


def row_to_columns(row):
    return jnp.broadcast_to(row, (HD, row.shape[1])).T


def rows_to_row(block):
    return jnp.sum(block.T, axis=0, keepdims=True)


def nt(a, b):
    return lax.dot_general(a, b, (((1,), (1,)), ((), ())), preferred_element_type=F32)


def nn(a, b):
    return jnp.dot(a, b, preferred_element_type=F32)


def call(kernel, outs, ins, smem=0, scratch=(), flops=0, aliases=None, vmem=24, space=None):
    nbytes = sum(int(np.prod(o.shape)) * o.dtype.itemsize for o in list(outs) + list(ins)[smem:])
    big = VM if space is None else space
    return pl.pallas_call(
        kernel,
        out_shape=tuple(jax.ShapeDtypeStruct(o.shape, o.dtype) for o in outs),
        in_specs=[SM] * smem + [big] * (len(ins) - smem),
        out_specs=tuple(VM for _ in outs),
        scratch_shapes=list(scratch),
        input_output_aliases=aliases or {},
        compiler_params=pltpu.CompilerParams(vmem_limit_bytes=vmem << 20),
        cost_estimate=pl.CostEstimate(flops=flops, bytes_accessed=nbytes, transcendentals=0),
    )(*ins)


def in_hbm(x):
    return pltpu.with_memory_space_constraint(x, pltpu.HBM)


def shaped(shape, dtype):
    return jax.ShapeDtypeStruct(shape, dtype)


def head_of(tab, device):
    head = jnp.int32(-1)
    for d, h in enumerate(tab):
        if h >= 0:
            head = jnp.where(device == d, jnp.int32(h), head)
    return head


def head_at(me, tab, chips, half, c):
    return head_of(tab, me[0] ^ (half * chips + c))


def pack(me, tab, chips, source, mine, other):
    rows = source.shape[0]
    for half, out in ((0, mine), (1, other)):
        for c in range(chips):
            col = columns(jnp.maximum(head_at(me, tab, chips, half, c), 0))
            out[c * rows : (c + 1) * rows] = source[:, col]


def squares(ref):
    total = None
    for i in range(ref.shape[1] // HD):
        x = ref[:, tile(i)].astype(F32)
        total = x * x if total is None else total + x * x
    return total


def first_kernel(tab, chips, me, q_hbm, k_hbm, t_hbm, v_hbm, tv_hbm, mine, other, sums, q, k, t, v, sems):
    tokens = v_hbm.shape[0]
    copies = []
    pairs = [(v_hbm, v.at[:tokens]), (tv_hbm, v.at[tokens:]), (k_hbm, k), (q_hbm, q), (t_hbm, t)]
    for i, (a, b) in enumerate(pairs):
        copies.append(pltpu.make_async_copy(a, b, sems.at[i]))
        copies[-1].start()
    copies[0].wait()
    copies[1].wait()
    pack(me, tab, chips, v, mine, other)
    for copy in copies[2:]:
        copy.wait()
    parts = [squares(q), squares(k), squares(t)]
    rest = sums.shape[1] - sum(p.shape[0] for p in parts)
    if rest:
        parts.append(jnp.zeros((rest, HD), F32))
    sums[...] = rows_to_row(jnp.concatenate(parts, axis=0))


def merge_kernel(chips, mine, other, *outs):
    rows = mine.shape[0] // chips
    for c, out in enumerate(outs):
        out[:rows] = mine[c * rows : (c + 1) * rows]
        out[rows:] = other[c * rows : (c + 1) * rows]


def send_k_kernel(tab, width, count, chips, me, *refs):
    sums, (k, tk, gain, mine, other, scales, normed) = refs[:count], refs[count:]
    tokens, texts = k.shape[0], tk.shape[0]
    scale = lax.rsqrt(total_of(sums) * (1.0 / width) + EPS)
    scales[...] = scale
    cols = row_to_columns(scale[:, tokens:])
    for i in range(k.shape[1] // HD):
        g = gain[:, tile(i)]
        normed[:tokens, tile(i)] = (k[:, tile(i)].astype(F32) * cols[:tokens] * g).astype(BF)
        normed[tokens:, tile(i)] = (
            tk[:, tile(i)].astype(F32) * cols[tokens : tokens + texts] * g
        ).astype(BF)
    pack(me, tab, chips, normed, mine, other)


def send_q_kernel(tab, chips, me, vid, scales, q, gain, cot, mine, other, both):
    tokens = q.shape[0]
    cols = row_to_columns(scales[:, :tokens])
    row = me[0] * tokens + lax.broadcasted_iota(jnp.int32, (tokens, HD), 0)
    live = row < vid[0]
    for i in range(q.shape[1] // HD):
        g = gain[:, tile(i)]
        both[:tokens, tile(i)] = (q[:, tile(i)].astype(F32) * cols * g).astype(BF)
        both[tokens:, tile(i)] = jnp.where(live, cot[:, tile(i)].astype(F32), 0.0).astype(BF)
    pack(me, tab, chips, both, mine, other)


def places(members, tokens, texts, source):
    text_at = pl.ds(pl.multiple_of(source * texts, texts), texts)
    video_at = pl.ds(pl.multiple_of(members * texts + source * tokens, texts), tokens)
    return text_at, video_at


def assemble_kernel(chips, texts, me, *refs):
    pieces_v, pieces_k = refs[:chips], refs[chips : 2 * chips]
    k, v, kt, vt = refs[2 * chips :]
    span = pieces_v[0].shape[0] // 2
    tokens = span - texts
    for pieces, whole in ((pieces_k, k), (pieces_v, v)):
        for c in range(chips):
            for half in (0, 1):
                source = me[0] ^ (half * chips + c)
                text_at, video_at = places(2 * chips, tokens, texts, source)
                whole[text_at] = pieces[c][half * span + tokens : (half + 1) * span]
                whole[video_at] = pieces[c][half * span : half * span + tokens]
    for whole, turned in ((k, kt), (v, vt)):
        step = 256
        for start in range(0, whole.shape[0], step):
            turned[:, start : start + step] = whole[start : start + step, :].T


def attention_kernel(tab, spec, me, vid, txt, query, k, v, kt, vt, *refs):
    chips, tokens, texts, c, step = spec
    out, dk, dv, gains, dots, scores, weights, top, totals, turned_out, turned_dq = refs
    scale = HD ** (-0.5)
    span = 2 * chips * texts
    rows = k.shape[0]
    videos = rows - span
    blocks = [slice(start, start + step) for start in range(0, rows, step)]
    low_text, low_video = span * 3 // 4, span + videos // 2

    gains[...] = jnp.zeros_like(gains)
    dots[...] = jnp.zeros_like(dots)

    def masked(s, start):
        parts = []
        for begin, end, limit in (
            (0, low_text, None),
            (low_text, span, txt[0]),
            (span, low_video, None),
            (low_video, rows, span + vid[0]),
        ):
            begin, end = max(begin, start), min(end, start + step)
            if begin >= end:
                continue
            part = s[begin - start : end - start]
            if limit is not None:
                row = lax.broadcasted_iota(jnp.int32, part.shape, 0)
                part = jnp.where(row < limit - begin, part, NEG)
            parts.append(part)
        return parts[0] if len(parts) == 1 else jnp.concatenate(parts, axis=0)

    def piece(half, unused):
        source = me[0] ^ (half * chips + c)
        active = jnp.logical_and(head_of(tab, me[0]) >= 0, source * tokens < vid[0])
        q_at = pl.ds(pl.multiple_of(half * 2 * tokens, tokens), tokens)
        grad_at = pl.ds(pl.multiple_of(half * 2 * tokens + tokens, tokens), tokens)

        @pl.when(jnp.logical_not(active))
        def _():
            out[q_at] = jnp.zeros((tokens, HD), BF)
            out[grad_at] = jnp.zeros((tokens, HD), BF)

            @pl.when(half == 0)
            def _():
                dk[...] = jnp.zeros_like(dk)
                dv[...] = jnp.zeros_like(dv)

        def work(add):
            q = query[q_at]
            grad = query[grad_at]
            for i, at in enumerate(blocks):
                s = masked(nt(k[at], q), at.start)
                scores[at] = s
                most = jnp.max(s.reshape(step // 8, 8, tokens), axis=0)
                top[...] = most if i == 0 else jnp.maximum(top[...], most)
            highest = jnp.max(top[...], axis=0, keepdims=True) * (scale * LOG2E)
            for i, at in enumerate(blocks):
                p = jnp.exp2(scores[at] * (scale * LOG2E) - highest)
                part = jnp.sum(p.reshape(step // 8, 8, tokens), axis=0)
                low = p.astype(BF)
                weights[at] = low
                o = nn(vt[:, at], low)
                totals[...] = part if i == 0 else totals[...] + part
                turned_out[...] = o if i == 0 else turned_out[...] + o
            inverse = 1.0 / jnp.sum(totals[...], axis=0, keepdims=True)
            attention = turned_out[...] * inverse
            turned_grad = grad.astype(F32).T
            inner = jnp.sum(attention * turned_grad, axis=0, keepdims=True)
            inv_cols = row_to_columns(inverse)
            low_grad = (grad.astype(F32) * inv_cols).astype(BF)
            low_q = (q.astype(F32) * (inv_cols * scale)).astype(BF)
            out[q_at] = attention.T.astype(BF)
            for i, at in enumerate(blocks):
                p = weights[at]
                dp = nt(v[at], grad)
                ds = p * (dp - inner).astype(BF)
                dv_part, dk_part = nn(p, low_grad), nn(ds, low_q)
                dv[at] = jnp.where(add, dv[at], 0.0) + dv_part
                dk[at] = jnp.where(add, dk[at], 0.0) + dk_part
                dq = nn(kt[:, at], ds)
                turned_dq[...] = dq if i == 0 else turned_dq[...] + dq
            dq = (turned_dq[...] * (inverse * scale)).T
            out[grad_at] = dq.astype(BF)
            part = dq * q.astype(F32)
            gains[...] += jnp.sum(part.reshape(tokens // 8, 8, HD), axis=0)
            dots[:, pl.ds(pl.multiple_of(half * tokens, tokens), tokens)] = rows_to_row(part)

        @pl.when(active)
        def _():
            work(half > 0)

        return unused

    lax.fori_loop(0, 2, piece, 0)


def attention_scratch(keys, tokens):
    return [
        pltpu.VMEM((keys, tokens), F32),
        pltpu.VMEM((keys, tokens), BF),
        pltpu.VMEM((8, tokens), F32),
        pltpu.VMEM((8, tokens), F32),
        pltpu.VMEM((HD, tokens), F32),
        pltpu.VMEM((HD, tokens), F32),
    ]


def split_rows(lines, rest):
    block = jnp.concatenate(lines, axis=0)
    high = block.astype(BF).astype(F32)
    both = [high, block - high]
    if rest:
        both.append(jnp.zeros((rest, HD), F32))
    return jnp.concatenate(both, axis=0).astype(BF)


def pack_v_kernel(chips, texts, order, me, k, *refs):
    dks, dvs, gains = refs[:chips], refs[chips : 2 * chips], refs[2 * chips : 3 * chips]
    query_dots, refs = refs[3 * chips : 4 * chips], refs[4 * chips :]
    outs, dk, dots, dv = refs[:chips], refs[chips], refs[chips + 1], refs[-1]
    span = outs[0].shape[0] // 2 - 16
    tokens = span - texts
    rows, step = k.shape[0], 512
    gk = jnp.zeros((8, HD), F32)
    for start in range(0, rows, step):
        at = slice(start, min(start + step, rows))
        total = functools.reduce(lambda a, b: a + b, [ref[at] for ref in dks])
        dk[at] = total
        part = total * k[at].astype(F32)
        dots[:, at] = rows_to_row(part)
        gk = gk + jnp.sum(part.reshape(part.shape[0] // 8, 8, HD), axis=0)
        dv[at] = functools.reduce(lambda a, b: a + b, [ref[at] for ref in dvs]).astype(BF)
    for c, ref in zip(order, query_dots, strict=True):
        for half in (0, 1):
            source = me[0] ^ (half * chips + c)
            at = pl.ds(pl.multiple_of(rows + source * tokens, HD), tokens)
            dots[:, at] = ref[:, half * tokens : (half + 1) * tokens]
    gq = functools.reduce(lambda a, b: a + b, [ref[...] for ref in gains])
    gq = jnp.sum(gq, axis=0, keepdims=True)
    lines = split_rows([gq, jnp.sum(gk, axis=0, keepdims=True)], 12)
    for c in range(chips):
        for half in (0, 1):
            source = me[0] ^ (half * chips + c)
            text_at, video_at = places(2 * chips, tokens, texts, source)
            base = half * (span + 16)
            outs[c][base : base + tokens] = dv[video_at]
            outs[c][base + tokens : base + span] = dv[text_at]
            outs[c][base + span : base + span + 16] = lines


def pack_k_kernel(chips, texts, count, me, dk, *refs):
    sums, outs, dots = refs[:count], refs[count:-1], refs[-1]
    dots[...] = total_of(sums)
    keys = dk.shape[0]
    text_total = 2 * chips * texts
    tokens = (keys - text_total) // (2 * chips)
    text_lines = [dots[:, tile(i)] for i in range(text_total // HD)]
    for c in range(chips):
        span = outs[c].shape[0] // 2
        for half in (0, 1):
            source = me[0] ^ (half * chips + c)
            text_at, video_at = places(2 * chips, tokens, texts, source)
            base = half * span
            outs[c][base : base + tokens] = dk[video_at].astype(BF)
            outs[c][base + tokens : base + tokens + texts] = dk[text_at].astype(BF)
            lines = list(text_lines)
            for first in (text_total, keys):
                for i in range(tokens // HD):
                    start = pl.multiple_of(first + source * tokens + i * HD, HD)
                    lines.append(dots[:, pl.ds(start, HD)])
            rest = span - tokens - texts - 2 * len(lines)
            outs[c][base + tokens + texts : base + span] = split_rows(lines, rest)


def split_kernel(chips, *refs):
    out = refs[chips]
    rows = out.shape[0] // chips
    for c in range(chips):
        out[c * rows : (c + 1) * rows] = refs[c][rows:]


def each_head(me, tab, chips, blocks, other, visit):
    rows = other.shape[0] // chips
    for half in (0, 1):
        for c in range(chips):
            head = head_at(me, tab, chips, half, c)

            @pl.when(head >= 0)
            def _():
                col = columns(jnp.maximum(head, 0))
                if half:
                    visit(col, other, c * rows)
                else:
                    visit(col, blocks[c], 0)


def gather_q_kernel(tab, chips, me, vid, *refs):
    blocks, other = refs[:chips], refs[chips]
    out, dq = refs[chips + 1 :]
    tokens = out.shape[0]
    row = me[0] * tokens + lax.broadcasted_iota(jnp.int32, (tokens, HD), 0)
    live = row < vid[0]

    def visit(col, ref, at):
        o = ref[at : at + tokens].astype(F32)
        out[:, col] = jnp.where(live, o, 0.0).astype(BF)
        dq[:, col] = ref[at + tokens : at + 2 * tokens]

    each_head(me, tab, chips, blocks, other, visit)


def total_of(refs):
    total = refs[0][...]
    for ref in refs[1:]:
        total = total + ref[...]
    return total


def gather_v_kernel(tab, chips, me, *refs):
    blocks, other = refs[:chips], refs[chips]
    q_gain, k_gain, out, text_out, dq_gain, dk_gain = refs[chips + 1 :]
    tokens, texts = out.shape[0], text_out.shape[0]

    def visit(col, ref, at):
        out[:, col] = ref[at : at + tokens]
        text_out[:, col] = ref[at + tokens : at + tokens + texts]
        lines = ref[at + tokens + texts : at + tokens + texts + 16].astype(F32)
        dq_gain[:, col] = (lines[0:1] + lines[2:3]) / q_gain[:, col]
        dk_gain[:, col] = (lines[1:2] + lines[3:4]) / k_gain[:, col]

    each_head(me, tab, chips, blocks, other, visit)


def finish_kernel(tab, width, chips, me, *refs):
    blocks, other = refs[:chips], refs[chips]
    scales, q, k, tk, dq, q_gain, k_gain = refs[chips + 1 : chips + 8]
    q_out, out, text_out, dk, sums, text_cols = refs[chips + 8 :]
    tokens, texts = k.shape[0], tk.shape[0]
    rows = tokens + texts
    text_lines, lines = 2 * chips * texts // HD, tokens // HD
    every = text_lines + 2 * lines
    sums[...] = jnp.zeros_like(sums)

    def visit(col, ref, at):
        dk[:, col] = ref[at : at + rows]
        block = ref[at + rows : at + rows + 2 * every].astype(F32)
        sums[:every] += block[:every] + block[every:]

    each_head(me, tab, chips, blocks, other, visit)
    columns_of = lambda first: [
        row_to_columns(sums[first + i : first + i + 1]) for i in range(lines)
    ]
    for i in range(text_lines):
        text_cols[i * HD : (i + 1) * HD] = row_to_columns(sums[i : i + 1])
    text_at = pl.ds(pl.multiple_of(me[0] * texts, texts), texts)
    dots = columns_of(text_lines) + [text_cols[text_at]]

    cols = row_to_columns(scales[:, tokens:])[:rows]
    back = jnp.concatenate(dots, axis=0) * (cols * cols) * (1.0 / width)
    q_cols = row_to_columns(scales[:, :tokens])
    q_back = jnp.concatenate(columns_of(text_lines + lines), axis=0)
    q_back = q_back * (q_cols * q_cols) * (1.0 / width)
    for i in range(k.shape[1] // HD):
        scaled = q_cols * (dq[:, tile(i)].astype(F32) * q_gain[:, tile(i)])
        q_out[:, tile(i)] = (scaled - q[:, tile(i)].astype(F32) * q_back).astype(BF)
        scaled = cols * (dk[:, tile(i)].astype(F32) * k_gain[:, tile(i)])
        out[:, tile(i)] = (scaled[:tokens] - k[:, tile(i)].astype(F32) * back[:tokens]).astype(BF)
        text_out[:, tile(i)] = (
            scaled[tokens:] - tk[:, tile(i)].astype(F32) * back[tokens:]
        ).astype(BF)


def local(q_raw, k_raw, values, text_k, text_v, q_gain, k_gain, cotangent, vid_len, txt_len):
    tokens, cols = q_raw.shape
    texts = text_k.shape[0]
    heads = cols // HD
    chips = lax.axis_size("ctx")
    members = 2 * chips
    parts = lax.axis_size("tp")
    width = cols * parts
    table = head_owners(members, chips, heads)
    span = tokens + texts
    keys = members * span
    text_total = members * texts
    pad = -(-(2 * tokens + texts) // HD) * HD
    extra = -(-2 * (text_total // HD + 2 * tokens // HD) // 16) * 16

    me = lax.axis_index(GROUP).astype(jnp.int32).reshape(1)
    tab = tuple(int(h) for h in table)
    qg = q_gain.reshape(1, cols)
    kg = k_gain.reshape(1, cols)

    def along(block, c, to_owner):
        if c == 0:
            return block
        pairs = [(s, s ^ c) for s in range(members) if table[s ^ c if to_owner else s] >= 0]
        return lax.ppermute(block, GROUP, pairs)

    def sibling(block):
        return lax.ppermute(block, "section", [(0, 1), (1, 0)])

    def shared(block):
        got = [block]
        for d in range(1, parts):
            got.append(lax.ppermute(block, "tp", [(s, s ^ d) for s in range(parts)]))
        return got

    far_first = far_chips(chips)
    chip_order = [0] + far_first[-1:] + far_first[:-1]

    def merged(mine, other):
        rows = mine.shape[0] // chips
        messages = call(
            functools.partial(merge_kernel, chips),
            [shaped((2 * rows, HD), BF)] * chips,
            [mine, sibling(other)],
        )
        got = {c: along(messages[c], c, True) for c in far_first}
        got[0] = messages[0]
        return [got[c] for c in range(chips)]

    mine_v, other_v, sums = call(
        functools.partial(first_kernel, tab, chips),
        [shaped((chips * span, HD), BF)] * 2 + [shaped((1, pad), F32)],
        [me] + [in_hbm(x) for x in (q_raw, k_raw, text_k, values, text_v)],
        smem=1,
        scratch=[
            pltpu.VMEM((tokens, cols), BF),
            pltpu.VMEM((tokens, cols), BF),
            pltpu.VMEM((texts, cols), BF),
            pltpu.VMEM((span, cols), BF),
            pltpu.SemaphoreType.DMA((5,)),
        ],
        space=pl.BlockSpec(memory_space=pltpu.HBM),
    )
    sums = shared(sums)
    got_v = merged(mine_v, other_v)
    mine_k, other_k, scales = call(
        functools.partial(send_k_kernel, tab, width, parts, chips),
        [shaped((chips * span, HD), BF)] * 2 + [shaped((1, pad), F32)],
        [me, *sums, k_raw, text_k, kg],
        smem=1,
        scratch=[pltpu.VMEM((span, cols), BF)],
    )
    got_k = merged(mine_k, other_k)
    mine_q, other_q = call(
        functools.partial(send_q_kernel, tab, chips),
        [shaped((chips * 2 * tokens, HD), BF)] * 2,
        [me, vid_len, scales, q_raw, qg, cotangent],
        smem=2,
        scratch=[pltpu.VMEM((2 * tokens, cols), BF)],
    )
    got_q = merged(mine_q, other_q)

    whole = call(
        functools.partial(assemble_kernel, chips, texts),
        [shaped((keys, HD), BF)] * 2 + [shaped((HD, keys), BF)] * 2,
        [me, *got_v, *got_k],
        smem=1,
    )

    back_q = {}
    dk_calls, dv_calls, gain_calls, dot_calls = [], [], [], []
    step = max(d for d in range(256, 1281, 128) if keys % d == 0)
    for c in chip_order:
        block, dk_call, dv_call, gain_call, dot_call = call(
            functools.partial(attention_kernel, tab, (chips, tokens, texts, c, step)),
            [shaped((4 * tokens, HD), BF)]
            + [shaped((keys, HD), F32)] * 2
            + [shaped((8, HD), F32), shaped((1, 2 * tokens), F32)],
            [me, vid_len, txt_len, got_q[c], *whole],
            smem=3,
            scratch=attention_scratch(keys, tokens),
            flops=6 * 2 * 2 * tokens * keys * HD * 2,
        )
        back_q[c] = along(block, c, False)
        dk_calls.append(dk_call)
        dv_calls.append(dv_call)
        gain_calls.append(gain_call)
        dot_calls.append(dot_call)
    *dv_parts, dk_sum, dots = call(
        functools.partial(pack_v_kernel, chips, texts, chip_order),
        [shaped((2 * (span + 16), HD), BF)] * chips
        + [shaped((keys, HD), F32), shaped((1, keys + members * tokens), F32)],
        [me, whole[0], *dk_calls, *dv_calls, *gain_calls, *dot_calls],
        smem=1,
        scratch=[pltpu.VMEM((keys, HD), BF)],
    )
    back_v = {c: along(dv_parts[c], c, False) for c in far_first + [0]}
    dots = shared(dots)
    dk_parts = call(
        functools.partial(pack_k_kernel, chips, texts, parts),
        [shaped((2 * (span + extra), HD), BF)] * chips,
        [me, dk_sum, *dots],
        smem=1,
        scratch=[pltpu.VMEM((1, keys + members * tokens), F32)],
    )
    back_k = {c: along(dk_parts[c], c, False) for c in far_first + [0]}

    def mine_and_other(back):
        blocks = [back[c] for c in range(chips)]
        rows = blocks[0].shape[0] // 2
        (other,) = call(
            functools.partial(split_kernel, chips), [shaped((chips * rows, HD), BF)], blocks
        )
        return [*blocks, sibling(other)]

    attention_out, dq = call(
        functools.partial(gather_q_kernel, tab, chips),
        [shaped((tokens, cols), BF)] * 2,
        [me, vid_len, *mine_and_other(back_q)],
        smem=2,
    )
    d_values, d_text_v, d_q_gain, d_k_gain = call(
        functools.partial(gather_v_kernel, tab, chips),
        [shaped((tokens, cols), BF), shaped((texts, cols), BF)] + [shaped((1, cols), F32)] * 2,
        [me, *mine_and_other(back_v), qg, kg],
        smem=1,
    )
    d_q_raw, d_k_raw, d_text_k = call(
        functools.partial(finish_kernel, tab, width, chips),
        [shaped((tokens, cols), BF)] * 2 + [shaped((texts, cols), BF)],
        [me, *mine_and_other(back_k), scales, q_raw, k_raw, text_k, dq, qg, kg],
        smem=1,
        scratch=[
            pltpu.VMEM((span, cols), BF),
            pltpu.VMEM((extra, HD), F32),
            pltpu.VMEM((text_total, HD), F32),
        ],
    )
    return (
        attention_out,
        d_q_raw,
        d_k_raw,
        d_values,
        d_text_k,
        d_text_v,
        d_q_gain.reshape(cols),
        d_k_gain.reshape(cols),
    )


def far_chips(chips):
    return sorted(range(1, chips), key=lambda c: (-c.bit_length(), c))


def solution(mesh):
    rows = P(GROUP, "tp")
    return jax.shard_map(
        local,
        mesh=mesh,
        in_specs=(rows,) * 5 + (P("tp"), P("tp"), rows, P(), P()),
        out_specs=(rows,) * 6 + (P("tp"), P("tp")),
        check_vma=False,
    )
```
